512 devices in a mesh: seq: 64 (over z, y), head: 8 (over x, core).
Axes of the slice: x: 4, y: 4, z: 16, core: 2. Of those that a mesh axis runs over, the one named last changes fastest.
Arguments:
- stream_x: bfloat16 [16384, 3072], P('seq', 'head')
- qkv_weight: bfloat16 [3072, 4608], P(None, 'head')
- short_lengths: int32 [32], replicated, may hold values from 1 to 256, 4096 in all
- cache_owner: int32 [16384, 1], P('seq'), may hold values from 0 to 63, as said below
Outputs:
- attended: bfloat16 [16384, 1536], P('seq', 'head')
- row_lse: float32 [16, 16384], P('head', 'seq')
- kv_cache: bfloat16 [32768, 3072], P('seq', 'head')
The draws below stay inside these ranges and needn't reach their ends.
Inputs may be any that keep to these rules, and one draw needn't show every extreme that they name: `short_lengths`: the lengths sum to 4096 and the longest is exactly 256. `cache_owner`: the rows of one device form 256 / 8 aligned pages of 8 rows; all rows of a page name the same owner, and the pages of one device name different owners, so an owner takes either none or exactly 8 rows of one device.
All inputs are finite; a program needn't handle non-finite values.
Results may differ from the reference program's by a relative error of at most 0.0083.
Values may be sent and summed in bfloat16 or wider, within the bound.
No kernel may reach another device: no remote copies, remote signals or barrier semaphores. Data moves between devices by JAX's collectives and lax.ppermute only.
A program may use at most 128 MiB of HBM per device.

```python
import math
import jax
import jax.numpy as jnp
import numpy as np
from jax import lax

D = 3072
HD = 96
HEADS = 16
TOK_DEV = 256
STREAM = 16384
LONG = 11264
NSHORT = 32
SHORT_SUM = 4096
CAP = 8
ROWS_OWNER = 512
CACHE_ROWS = 32768
N_SEQ = 64


def draw_stream_x(key, part):
    first_key = jax.random.fold_in(key, 0)
    drawn = jax.random.normal(first_key, (STREAM, D), jnp.float32)
    return jnp.clip(drawn, -6.0, 6.0).astype(jnp.bfloat16)


def draw_qkv_weight(key, part):
    first_key = jax.random.fold_in(key, 0)
    drawn = jax.random.normal(first_key, (D, HEADS, 3, HD), jnp.float32) * D ** (-0.5)
    return drawn.reshape(D, HEADS * 3 * HD).astype(jnp.bfloat16)


def draw_cache_owner(key, part):
    owner_key = jax.random.fold_in(key, 7)
    device_keys = jax.random.split(owner_key, N_SEQ)
    pages_dev = TOK_DEV // CAP

    def page_owners(device_key):
        return jax.random.permutation(device_key, N_SEQ)[:pages_dev].astype(jnp.int32)
    owners = jax.vmap(page_owners)(device_keys)
    rows = jnp.repeat(owners[:, :, None], CAP, axis=2)
    return rows.reshape(STREAM, 1).astype(jnp.int32)


def profile(number_of, total, reach, slope):
    weights = [(1 << 20) // math.isqrt(rank ** slope) + 1 for rank in range(2, number_of + 1)]
    spare, counts = total - reach - (number_of - 1), [1] * (number_of - 1)
    while spare > 0:
        movable = [i for i in range(number_of - 1) if counts[i] < reach]
        mass, remaining = sum([weights[i] for i in movable]), spare
        for i in movable:
            extra = min(reach - counts[i], max(1, remaining * weights[i] // mass), spare)
            counts[i] = counts[i] + extra
            spare = spare - extra
    return np.array([reach] + counts)


def ragged_sizes(rng, amount, total, reach, skew):
    if amount == 2:
        one = jax.random.randint(rng, (), max(1, total - reach), min(reach, total - 1) + 1)
        return jnp.stack([one, total - one])
    lengths = jnp.asarray(profile(amount, total, reach, skew), jnp.int32)
    pairs = (amount - 1) // 2
    giver, sink = lengths[1:1 + 2 * pairs:2], lengths[2:2 + 2 * pairs:2]
    room = jnp.minimum(giver - 1, reach - sink)
    shifted = jax.random.randint(jax.random.fold_in(rng, 1), (pairs,), 0, 1 << 20) % (room + 1)
    lengths = lengths.at[1:1 + 2 * pairs:2].set(giver - shifted).at[2:2 + 2 * pairs:2].set(sink + shifted)
    return lengths[jax.random.permutation(jax.random.fold_in(rng, 2), amount)]


def setup_inputs(seed: int = 0) -> dict:
    seeds = jax.random.split(jax.random.key(seed), 5)
    stream_x = draw_stream_x(jax.random.fold_in(seeds[4], 71), 0)
    qkv_weight = draw_qkv_weight(jax.random.fold_in(seeds[4], 71), 0)
    short_lengths = ragged_sizes(seeds[2], NSHORT, SHORT_SUM, TOK_DEV, 2).astype(jnp.int32)
    cache_owner = draw_cache_owner(jax.random.fold_in(seeds[4], 71), 0)
    return {"stream_x": stream_x, "qkv_weight": qkv_weight, "short_lengths": short_lengths, "cache_owner": cache_owner}


neg_large = -1e+30
rope_base = 10000.0

def boundaries(short_lengths):
    running = jnp.cumsum(short_lengths.astype(jnp.int32)).astype(jnp.int32)
    return (jnp.concatenate([jnp.zeros((1,), jnp.int32), running]) + LONG).astype(jnp.int32)

def locate(row_ids, bounds):
    passed = row_ids[:, None] >= bounds[None, :]
    segment = lax.optimization_barrier(jnp.sum(passed.astype(jnp.int32), axis=1)).astype(jnp.int32)
    seg_begin = lax.optimization_barrier(jnp.max(jnp.where(passed, bounds[None, :], 0), axis=1)).astype(jnp.int32)
    return (segment, seg_begin)

def segment_at(row_id, bounds):
    return jnp.sum((row_id >= bounds).astype(jnp.int32)).astype(jnp.int32)

def rotate(parts, position, head_dim):
    half_dim = head_dim // 2
    inverse_freq = rope_base ** (-jnp.arange(half_dim, dtype=jnp.float32) / half_dim)
    angle = position[:, None, None] * inverse_freq[None, None, :]
    cosine = jnp.cos(angle)
    sine_part = jnp.sin(angle)
    first_half = parts[..., :half_dim]
    second_half = parts[..., half_dim:]
    return jnp.concatenate([first_half * cosine - second_half * sine_part, second_half * cosine + first_half * sine_part], axis=-1)

def reference(stream_x, qkv_weight, short_lengths, cache_owner):
    bounds = boundaries(short_lengths)
    row_ids = jnp.arange(STREAM, dtype=jnp.int32)
    segment, seg_begin = locate(row_ids, bounds)
    position = (row_ids - seg_begin).astype(jnp.float32)
    is_padding = segment == NSHORT + 1
    projected = jnp.dot(stream_x, qkv_weight, preferred_element_type=jnp.float32).reshape(STREAM, HEADS, 3, HD)
    queries = rotate(projected[:, :, 0], position, HD).astype(jnp.bfloat16)
    rotated_keys = rotate(projected[:, :, 1], position, HD).astype(jnp.bfloat16)
    values = projected[:, :, 2].astype(jnp.bfloat16)
    query_heads = jnp.transpose(queries, (1, 0, 2))
    key_heads = jnp.transpose(rotated_keys, (1, 0, 2))
    value_heads = jnp.transpose(values, (1, 0, 2))
    block_rows = min(512, STREAM)
    block_count = STREAM // block_rows
    score_scale = 1.0 / math.sqrt(HD)

    def attend(head_index, block_index):
        first_row = (block_index * block_rows).astype(jnp.int32)
        query_block = lax.dynamic_slice_in_dim(query_heads[head_index], first_row, block_rows, 0)
        query_ids = first_row + jnp.arange(block_rows, dtype=jnp.int32)
        query_segment = lax.dynamic_slice_in_dim(segment, first_row, block_rows, 0)
        low_segment = segment_at(first_row, bounds)

        def scan_step(running, key_index):
            key_first = (key_index * block_rows).astype(jnp.int32)
            last_segment = segment_at(key_first + block_rows - 1, bounds)
            relevant = (key_first <= first_row + block_rows - 1) & (last_segment >= low_segment)

            def compute(partial_value):
                row_max, denominator, context = partial_value
                key_block = lax.dynamic_slice_in_dim(key_heads[head_index], key_first, block_rows, 0)
                value_block = lax.dynamic_slice_in_dim(value_heads[head_index], key_first, block_rows, 0)
                key_ids = key_first + jnp.arange(block_rows, dtype=jnp.int32)
                key_segment = lax.dynamic_slice_in_dim(segment, key_first, block_rows, 0)
                scores = jnp.dot(query_block, key_block.T, preferred_element_type=jnp.float32) * score_scale
                allowed = (key_segment[None, :] == query_segment[:, None]) & (key_ids[None, :] <= query_ids[:, None])
                new_max = jnp.maximum(row_max, lax.optimization_barrier(jnp.max(jnp.where(allowed, scores, neg_large), axis=1)))
                factor = jnp.exp(row_max - new_max)
                weights = jnp.where(allowed, jnp.exp(scores - new_max[:, None]), 0.0)
                denominator = factor * denominator + lax.optimization_barrier(jnp.sum(weights, axis=1))
                context = factor[:, None] * context + jnp.dot(weights.astype(jnp.bfloat16), value_block, preferred_element_type=jnp.float32)
                return (new_max, denominator, context)
            return (lax.cond(relevant, compute, lambda partial_value: partial_value, running), None)
        start_state = (jnp.full((block_rows,), neg_large, jnp.float32), jnp.zeros((block_rows,), jnp.float32), jnp.zeros((block_rows, HD), jnp.float32))
        final_state, unused = lax.scan(scan_step, start_state, jnp.arange(block_count, dtype=jnp.int32))
        row_max, denominator, context = final_state
        return (context / denominator[:, None], row_max + jnp.log(denominator))

    def per_head(head_index):
        return lax.map(lambda block_index: attend(head_index, block_index), jnp.arange(block_count, dtype=jnp.int32))
    context, log_total = lax.map(per_head, jnp.arange(HEADS, dtype=jnp.int32))
    context = context.reshape(HEADS, STREAM, HD)
    log_total = log_total.reshape(HEADS, STREAM)
    context = jnp.where(is_padding[None, :, None], 0.0, context)
    row_lse = jnp.where(is_padding[None, :], 0.0, log_total)
    attended = jnp.transpose(context, (1, 0, 2)).reshape(STREAM, HEADS * HD).astype(jnp.bfloat16)
    owner_ids = cache_owner[:, 0]
    one_hot = (owner_ids.reshape(N_SEQ, TOK_DEV)[:, :, None] == jnp.arange(N_SEQ, dtype=jnp.int32)[None, None, :]).astype(jnp.int32)
    owner_rank = (lax.optimization_barrier(jnp.sum(jnp.cumsum(one_hot, axis=1) * one_hot, axis=2)) - 1).reshape(STREAM)
    source = row_ids // TOK_DEV
    slot_index = (owner_ids * ROWS_OWNER + source * CAP + owner_rank).astype(jnp.int32)
    packed = jnp.stack([rotated_keys, values], axis=2).reshape(STREAM, HEADS * 2 * HD)
    cached = jnp.where(is_padding[:, None], jnp.zeros_like(packed), packed)
    kv_cache = jnp.zeros((CACHE_ROWS, HEADS * 2 * HD), jnp.bfloat16).at[slot_index].set(cached)
    return (attended, row_lse, kv_cache)
```

```python
import functools
import math

import jax
import jax.numpy as jnp
from jax import lax
from jax.experimental import pallas as pl
from jax.experimental.pallas import tpu as pltpu
from jax.sharding import Mesh, PartitionSpec as P

HD = 96
CAP = 8
neg_large = -1e30
rope_base = 10000.0
score_scale = 1.0 / math.sqrt(HD)
log2_scale = score_scale * math.log2(math.e)


def boundaries(short_lengths, long_length):
    running = jnp.cumsum(short_lengths)
    return jnp.concatenate([jnp.zeros((1,), jnp.int32), running]) + long_length


def locate(row_ids, bounds):
    passed = row_ids[:, None] >= bounds[None, :]
    segment = jnp.sum(passed.astype(jnp.int32), axis=1)
    seg_begin = jnp.max(jnp.where(passed, bounds[None, :], 0), axis=1)
    return (segment, seg_begin)


def lane_ids(shape):
    return lax.broadcasted_iota(jnp.int32, shape, 1)


def half_projection(core_ref, x_ref, w_ref, out_ref):
    step = pl.program_id(0)
    part = jnp.dot(x_ref[0], w_ref[...], preferred_element_type=jnp.float32)

    @pl.when(step == 0)
    def _():
        out_ref[...] = part

    @pl.when(step > 0)
    def _():
        out_ref[...] += part


def pack_heads(p0, p1, p2, p3):
    lanes = lane_ids(p0.shape)
    r1 = pltpu.roll(p1, 96, 1)
    r2 = pltpu.roll(p2, 64, 1)
    r3 = pltpu.roll(p3, 32, 1)
    return (
        jnp.where(lanes < 96, p0, r1),
        jnp.where(lanes < 64, r1, r2),
        jnp.where(lanes < 32, r2, r3),
    )


def rest_projection(core_ref, x_ref, w_ref, first_ref, cos_ref, sin_ref, map_ref, q_ref, kv_ref, acc):
    step = pl.program_id(0)
    part = jnp.dot(x_ref[0], w_ref[...], preferred_element_type=jnp.float32)

    @pl.when(step == 0)
    def _():
        acc[:, :576] = first_ref[...] + part
        acc[:, 576:] = jnp.zeros_like(acc[:, 576:])

    @pl.when(step > 0)
    def _():
        acc[:, :576] += part

    @pl.when(step == pl.num_programs(0) - 1)
    def _():
        whole = acc[...]
        cosine = cos_ref[...]
        sine = sin_ref[...]
        lanes = lane_ids((whole.shape[0], 128))
        width = whole.shape[1]

        def window(first):
            return pltpu.roll(whole, (width - first) % width, 1)[:, :128]

        def rotated(first):
            here = window(first)
            ahead = window(first + 48)
            behind = window((first - 48) % width)
            return here * cosine + jnp.where(lanes < 48, ahead, behind) * sine

        def plain(first):
            return jnp.where(lanes < HD, window(first), 0.0)

        zero = jnp.zeros((whole.shape[0], 128), jnp.float32)
        queries = pack_heads(rotated(0), zero, rotated(288), zero)
        key_values = pack_heads(rotated(96), plain(192), rotated(384), plain(480))
        rows = q_ref.shape[0]
        for i in range(3):
            q_ref[:, 128 * i : 128 * i + 128] = queries[i].astype(jnp.bfloat16)
            kv_ref[:rows, 128 * i : 128 * i + 128] = key_values[i].astype(jnp.bfloat16)
        kv_ref[rows:, :] = jnp.broadcast_to(map_ref[...], (kv_ref.shape[0] - rows, 384)).astype(
            jnp.bfloat16
        )


def select_pages(table_ref, pages_ref, out_ref):
    targets, sources = out_ref.shape[:2]

    def one(i, carry):
        target = i % targets
        source = i // targets
        page = table_ref[i]
        rows = pages_ref[source, jnp.maximum(page, 0)]
        out_ref[target, source] = jnp.where(page >= 0, rows, jnp.zeros_like(rows))
        return carry

    lax.fori_loop(0, targets * sources, one, 0)


def attention(info_ref, q_ref, begin_ref, kv_ref, out_ref, scores):
    plane, column, low, masked_low = info_ref[0], info_ref[1], info_ref[2], info_ref[3]
    rows = q_ref.shape[0]
    keys = 256
    chunk = scores.shape[1]
    lanes = lane_ids((chunk, 128))

    for head in range(2):
        col = 0 if head == 0 else 128
        width = 128 if head == 0 else 256
        vcol = 0 if head == 0 else 256
        vwidth = 256 if head == 0 else 128
        for first in range(0, rows, chunk):
            q = q_ref[first : first + chunk, col : col + width]
            row_ids = plane * rows + first + lax.broadcasted_iota(jnp.int32, (chunk, keys), 0)

            def raw(j):
                k = kv_ref[j, :keys, col : col + width]
                return lax.dot_general(
                    q, k, (((1,), (1,)), ((), ())), preferred_element_type=jnp.float32
                )

            def fold(s):
                return jnp.maximum(s[:, :128], s[:, 128:])

            def free(j, top):
                s = raw(j)
                scores[j - low] = s
                return jnp.maximum(top, fold(s))

            def masked(j, top):
                key_ids = (
                    j * rows + column * keys + lax.broadcasted_iota(jnp.int32, (chunk, keys), 1)
                )
                begin = begin_ref[first : first + chunk, :]
                allowed = (key_ids <= row_ids) & (key_ids >= begin)
                s = jnp.where(allowed, raw(j), neg_large)
                scores[j - low] = s
                return jnp.maximum(top, fold(s))

            top = jnp.full((chunk, 128), neg_large, jnp.float32)
            top = lax.fori_loop(low, masked_low, free, top)
            top = lax.fori_loop(masked_low, plane + 1, masked, top)
            peak = jnp.max(top, axis=1, keepdims=True)

            def weigh(j, state):
                total, context = state
                p = jnp.exp2((scores[j - low] - peak) * log2_scale)
                v = kv_ref[j, :keys, vcol : vcol + vwidth]
                total = total + (p[:, :128] + p[:, 128:])
                context = context + jnp.dot(
                    p.astype(jnp.bfloat16), v, preferred_element_type=jnp.float32
                )
                return total, context

            total, context = lax.fori_loop(
                low,
                plane + 1,
                weigh,
                (
                    jnp.zeros((chunk, 128), jnp.float32),
                    jnp.zeros((chunk, vwidth), jnp.float32),
                ),
            )
            denominator = jnp.sum(total, axis=1, keepdims=True)
            if head == 0:
                left = pltpu.roll(context[:, :128], 32, 1)
                right = pltpu.roll(context[:, 128:], 32, 1)
                context = jnp.where(lanes < 32, left, right)
            else:
                context = pltpu.roll(context, 96, 1)
            context = context / denominator
            lse = peak * score_scale + jnp.log(denominator)
            coarse = lse.astype(jnp.bfloat16)
            rest = lse - coarse.astype(jnp.float32)
            middle = rest.astype(jnp.bfloat16)
            fine = rest - middle.astype(jnp.float32)
            packed = jnp.where(
                lanes < HD,
                context,
                jnp.where(
                    lanes == HD,
                    coarse.astype(jnp.float32),
                    jnp.where(lanes == HD + 1, middle.astype(jnp.float32), fine),
                ),
            )
            out_ref[first : first + chunk, head * 128 : head * 128 + 128] = packed.astype(
                jnp.bfloat16
            )


def combine(flag_ref, parts_ref, att_ref, lse_ref):
    count, rows = parts_ref.shape[:2]
    live = flag_ref[0] == 0
    heads = []
    for head in range(2):
        parts = [
            parts_ref[i, :, head * 128 : head * 128 + 128].astype(jnp.float32)
            for i in range(count)
        ]
        lses = [p[:, 96:97] + p[:, 97:98] + p[:, 98:99] for p in parts]
        peak = functools.reduce(jnp.maximum, lses)
        weights = [jnp.exp(v - peak) for v in lses]
        total = functools.reduce(jnp.add, weights)
        context = functools.reduce(jnp.add, [p * w for p, w in zip(parts, weights)])
        lanes = lane_ids(context.shape)
        context = jnp.where(live & (lanes < HD), context / total, 0.0)
        heads.append(context)
        lse = jnp.where(live, peak + jnp.log(total), 0.0)
        lse_ref[head : head + 1, :] = jnp.transpose(
            jnp.broadcast_to(lse, (rows, 128)), (1, 0)
        )[:1, :]
    lanes = lane_ids(heads[0].shape)
    moved = pltpu.roll(heads[1], 96, 1)
    att_ref[:, :128] = jnp.where(lanes < HD, heads[0], moved).astype(jnp.bfloat16)
    att_ref[:, 128:] = moved[:, :64].astype(jnp.bfloat16)


SMEM = pl.BlockSpec(memory_space=pltpu.SMEM)
VMEM = pl.BlockSpec(memory_space=pltpu.VMEM)


def project(core, gathered, weight, extra=None):
    blocks, rows, depth = gathered.shape
    columns = weight.shape[1]
    x_spec = pl.BlockSpec((1, rows, depth), lambda i, c: (i, 0, 0))
    w_spec = pl.BlockSpec((depth, columns), lambda i, c: (2 * i + c[0], 0))

    def fixed(shape):
        return pl.BlockSpec(shape, lambda i, c: (0,) * len(shape))

    if extra is None:
        return pl.pallas_call(
            half_projection,
            grid_spec=pltpu.PrefetchScalarGridSpec(
                num_scalar_prefetch=1,
                grid=(blocks,),
                in_specs=[x_spec, w_spec],
                out_specs=fixed((rows, columns)),
            ),
            out_shape=jax.ShapeDtypeStruct((rows, columns), jnp.float32),
        )(core, gathered, weight)
    first, cosine, sine, page_map = extra
    return pl.pallas_call(
        rest_projection,
        grid_spec=pltpu.PrefetchScalarGridSpec(
            num_scalar_prefetch=1,
            grid=(blocks,),
            in_specs=[
                x_spec,
                w_spec,
                fixed((rows, columns)),
                fixed((rows, 128)),
                fixed((rows, 128)),
                fixed((1, 384)),
            ],
            out_specs=[fixed((rows, 384)), fixed((rows + 16, 384))],
            scratch_shapes=[pltpu.VMEM((rows, 640), jnp.float32)],
        ),
        out_shape=[
            jax.ShapeDtypeStruct((rows, 384), jnp.bfloat16),
            jax.ShapeDtypeStruct((rows + 16, 384), jnp.bfloat16),
        ],
    )(core, gathered, weight, first, cosine, sine, page_map)


def body(stream_x, qkv_weight, short_lengths, cache_owner):
    planes, columns = lax.axis_size("z"), lax.axis_size("y")
    tok_count = stream_x.shape[0]
    plane, column = lax.axis_index("z"), lax.axis_index("y")
    core = lax.axis_index("c").astype(jnp.int32).reshape(1)
    plane_rows = tok_count * columns
    long_planes = planes * 11 // 16
    long_length = plane_rows * long_planes
    bounds = boundaries(short_lengths, long_length)
    pad_segment = short_lengths.shape[0] + 1

    ours = lax.all_gather(stream_x, "x", axis=0, tiled=False)
    theirs = lax.ppermute(ours, "c", [(0, 1), (1, 0)])

    first_row = plane * plane_rows + column * tok_count
    row_ids = first_row + jnp.arange(tok_count, dtype=jnp.int32)
    segment, seg_begin = locate(row_ids, bounds)
    position = (row_ids - seg_begin).astype(jnp.float32)
    half_dim = HD // 2
    inverse_freq = rope_base ** (-jnp.arange(half_dim, dtype=jnp.float32) / half_dim)
    angle = position[:, None] * inverse_freq[None, :]
    cosine = jnp.cos(angle)
    sine = jnp.sin(angle)
    blank = jnp.zeros((tok_count, 128 - HD), jnp.float32)
    cosine = jnp.concatenate([cosine, cosine, blank], axis=1)
    sine = jnp.concatenate([-sine, sine, blank], axis=1)

    pages = tok_count // CAP
    owners = planes * columns
    page_owner = cache_owner.reshape(pages, CAP)[:, 0]
    page_live = segment.reshape(pages, CAP)[:, 0] != pad_segment
    hit = (page_owner[:, None] == jnp.arange(owners, dtype=jnp.int32)[None, :]) & page_live[:, None]
    page_map = jnp.max(
        jnp.where(hit, jnp.arange(pages, dtype=jnp.int32)[:, None], -1), axis=0
    ).astype(jnp.float32)
    page_map = jnp.concatenate([page_map, jnp.zeros((384 - owners,), jnp.float32)])[None, :]

    half = project(core, ours, qkv_weight)
    queries, key_values = project(1 - core, theirs, qkv_weight, (half, cosine, sine, page_map))

    rows_sent = tok_count + 16
    gathered = lax.all_gather(key_values, "z", axis=0, tiled=True)
    plane_queries = lax.all_gather(queries, "y", axis=0, tiled=True)
    plane_ids = plane * plane_rows + jnp.arange(plane_rows, dtype=jnp.int32)
    unused, plane_begin = locate(plane_ids, bounds)

    is_long = plane < long_planes
    low = jnp.where(is_long, 0, jnp.maximum(plane - 1, long_planes))
    masked_low = jnp.where(is_long, plane, low)
    info = jnp.stack([plane, column, low, masked_low]).astype(jnp.int32)

    by_plane = gathered.reshape(planes, rows_sent, 384)
    table = lax.dynamic_slice_in_dim(
        by_plane[:, tok_count, :owners], plane * columns, columns, 1
    ).astype(jnp.int32)
    outbox = pl.pallas_call(
        select_pages,
        in_specs=[SMEM, VMEM],
        out_specs=VMEM,
        out_shape=jax.ShapeDtypeStruct((columns, planes, CAP, 384), jnp.bfloat16),
    )(table.reshape(-1), gathered.reshape(planes, rows_sent // CAP, CAP, 384))
    received = lax.all_to_all(
        outbox.reshape(columns, planes * CAP, 384), "y", split_axis=0, concat_axis=0, tiled=True
    )
    kv_cache = (
        received.reshape(columns, planes, CAP, 384)
        .transpose(1, 0, 2, 3)
        .reshape(planes * columns * CAP, 384)
    )

    chunk = 256
    partial = pl.pallas_call(
        attention,
        in_specs=[SMEM, VMEM, VMEM, VMEM],
        out_specs=VMEM,
        out_shape=jax.ShapeDtypeStruct((plane_rows, 256), jnp.bfloat16),
        scratch_shapes=[pltpu.VMEM((max(long_planes, 2), chunk, 256), jnp.float32)],
    )(info, plane_queries, plane_begin[:, None], by_plane)
    parts = lax.all_to_all(
        partial.reshape(columns, tok_count, 256), "y", split_axis=0, concat_axis=0, tiled=True
    )
    is_padding = (segment[:1] == pad_segment).astype(jnp.int32)
    attended, row_lse = pl.pallas_call(
        combine,
        in_specs=[SMEM, VMEM],
        out_specs=[VMEM, VMEM],
        out_shape=[
            jax.ShapeDtypeStruct((tok_count, 2 * HD), jnp.bfloat16),
            jax.ShapeDtypeStruct((2, tok_count), jnp.float32),
        ],
    )(is_padding, parts)
    return (attended, row_lse, kv_cache)


def solution(mesh):
    seq, head = mesh.devices.shape
    fine = Mesh(mesh.devices.reshape(seq // 4, 4, head // 2, 2), ("z", "y", "x", "c"))
    seq_axes, head_axes = ("z", "y"), ("x", "c")
    return jax.shard_map(
        body,
        mesh=fine,
        in_specs=(P(seq_axes, head_axes), P(None, head_axes), P(), P(seq_axes, None)),
        out_specs=(P(seq_axes, head_axes), P(head_axes, seq_axes), P(seq_axes, head_axes)),
        check_vma=False,
    )
```

```python
import functools
import math

import jax
import jax.numpy as jnp
from jax import lax
from jax.experimental import pallas as pl
from jax.experimental.pallas import tpu as pltpu
from jax.sharding import Mesh, PartitionSpec as P

HD = 96
CAP = 8
neg_large = -1e30
rope_base = 10000.0
score_scale = 1.0 / math.sqrt(HD)
log2_scale = score_scale * math.log2(math.e)


def boundaries(short_lengths, long_length):
    running = jnp.cumsum(short_lengths)
    return jnp.concatenate([jnp.zeros((1,), jnp.int32), running]) + long_length


def locate(row_ids, bounds):
    passed = row_ids[:, None] >= bounds[None, :]
    segment = jnp.sum(passed.astype(jnp.int32), axis=1)
    seg_begin = jnp.max(jnp.where(passed, bounds[None, :], 0), axis=1)
    return (segment, seg_begin)


def lane_ids(shape):
    return lax.broadcasted_iota(jnp.int32, shape, 1)


def half_projection(core_ref, x_ref, w_ref, out_ref):
    step = pl.program_id(0)
    part = lax.dot_general(
        x_ref[...], w_ref[...], (((1,), (1,)), ((), ())), preferred_element_type=jnp.float32
    )

    @pl.when(step == 0)
    def _():
        out_ref[...] = part

    @pl.when(step > 0)
    def _():
        out_ref[...] += part


def pack_heads(p0, p1, p2, p3):
    lanes = lane_ids(p0.shape)
    r1 = pltpu.roll(p1, 96, 1)
    r2 = pltpu.roll(p2, 64, 1)
    r3 = pltpu.roll(p3, 32, 1)
    return (
        jnp.where(lanes < 96, p0, r1),
        jnp.where(lanes < 64, r1, r2),
        jnp.where(lanes < 32, r2, r3),
    )


def rest_projection(core_ref, x_ref, w_ref, first_ref, cos_ref, sin_ref, map_ref, q_ref, kv_ref, acc):
    step = pl.program_id(0)
    part = lax.dot_general(
        x_ref[...], w_ref[...], (((1,), (1,)), ((), ())), preferred_element_type=jnp.float32
    )

    @pl.when(step == 0)
    def _():
        acc[:, :576] = first_ref[...] + part
        acc[:, 576:] = jnp.zeros_like(acc[:, 576:])

    @pl.when(step > 0)
    def _():
        acc[:, :576] += part

    @pl.when(step == pl.num_programs(0) - 1)
    def _():
        whole = acc[...]
        cosine = cos_ref[...]
        sine = sin_ref[...]
        lanes = lane_ids((whole.shape[0], 128))
        width = whole.shape[1]

        def window(first):
            return pltpu.roll(whole, (width - first) % width, 1)[:, :128]

        def rotated(first):
            here = window(first)
            ahead = window(first + 48)
            behind = window((first - 48) % width)
            return here * cosine + jnp.where(lanes < 48, ahead, behind) * sine

        def plain(first):
            return jnp.where(lanes < HD, window(first), 0.0)

        zero = jnp.zeros((whole.shape[0], 128), jnp.float32)
        queries = pack_heads(rotated(0), zero, rotated(288), zero)
        key_values = pack_heads(rotated(96), plain(192), rotated(384), plain(480))
        rows = q_ref.shape[0]
        for i in range(3):
            q_ref[:, 128 * i : 128 * i + 128] = queries[i].astype(jnp.bfloat16)
            kv_ref[:rows, 128 * i : 128 * i + 128] = key_values[i].astype(jnp.bfloat16)
        kv_ref[rows:, :] = jnp.broadcast_to(map_ref[...], (kv_ref.shape[0] - rows, 384)).astype(
            jnp.bfloat16
        )


def select_pages(table_ref, pages_ref, out_ref):
    targets, sources = out_ref.shape[:2]

    def one(i, carry):
        target = i % targets
        source = i // targets
        page = table_ref[i]
        rows = pages_ref[source, jnp.maximum(page, 0)]
        out_ref[target, source] = jnp.where(page >= 0, rows, jnp.zeros_like(rows))
        return carry

    lax.fori_loop(0, targets * sources, one, 0)


def attention(info_ref, q_ref, begin_ref, kv_ref, out_ref, scores, peaks, totals, contexts):
    plane, column, low, masked_low = info_ref[0], info_ref[1], info_ref[2], info_ref[3]
    rows = q_ref.shape[0]
    keys = 256
    chunk = 256
    planes = kv_ref.shape[0]
    count = plane + 1 - low
    parts = [
        (head, pl.ds(first, chunk), first) for head in range(2) for first in range(0, rows, chunk)
    ]
    key_cols = (slice(0, 128), slice(128, 384))
    value_cols = (slice(0, 256), slice(256, 384))
    value_width = (256, 128)

    def score(j, masked):
        for head, span, first in parts:
            s = lax.dot_general(
                q_ref[span, key_cols[head]],
                kv_ref[j, :keys, key_cols[head]],
                (((1,), (1,)), ((), ())),
                preferred_element_type=jnp.float32,
            )
            if masked:
                shape = (chunk, keys)
                row_ids = plane * rows + first + lax.broadcasted_iota(jnp.int32, shape, 0)
                key_ids = j * rows + column * keys + lax.broadcasted_iota(jnp.int32, shape, 1)
                allowed = (key_ids <= row_ids) & (key_ids >= begin_ref[span, :])
                s = jnp.where(allowed, s, neg_large)
            scores[j - low, head, span, :] = s
            peaks[head, span, :] = jnp.maximum(
                peaks[head, span, :], jnp.maximum(s[:, :128], s[:, 128:])
            )

    peaks[...] = jnp.full_like(peaks, neg_large)
    totals[...] = jnp.zeros_like(totals)
    contexts[...] = jnp.zeros_like(contexts)

    def free_step(j, carry):
        score(j, False)
        return carry

    def masked_step(j, carry):
        score(j, True)
        return carry

    lax.fori_loop(low, masked_low, free_step, 0)
    lax.fori_loop(masked_low, plane + 1, masked_step, 0)

    @pl.when(count % 2 == 1)
    def _():
        scores[count] = jnp.full(scores.shape[1:], neg_large, jnp.float32)

    tops = []
    for head, span, first in parts:
        top = jnp.max(peaks[head, span, :], axis=1, keepdims=True)
        tops.append(top)
        peaks[head, span, :] = jnp.broadcast_to(top * log2_scale, (chunk, 128))

    def weigh(i, carry):
        for head, span, first in parts:
            shift = peaks[head, span, :]
            total = totals[head, span, :]
            context = contexts[head, span, : value_width[head]]
            for k in range(2):
                slot = 2 * i + k
                j = jnp.minimum(low + slot, planes - 1)
                s = scores[slot, head, span, :]
                left = jnp.exp2(s[:, :128] * log2_scale - shift)
                right = jnp.exp2(s[:, 128:] * log2_scale - shift)
                total = total + (left + right)
                p = jnp.concatenate([left.astype(jnp.bfloat16), right.astype(jnp.bfloat16)], axis=1)
                context = context + jnp.dot(
                    p, kv_ref[j, :keys, value_cols[head]], preferred_element_type=jnp.float32
                )
            totals[head, span, :] = total
            contexts[head, span, : value_width[head]] = context
        return carry

    lax.fori_loop(0, (count + 1) // 2, weigh, 0)

    lanes = lane_ids((chunk, 128))
    for (head, span, first), top in zip(parts, tops):
        denominator = jnp.sum(totals[head, span, :], axis=1, keepdims=True)
        if head == 0:
            left = pltpu.roll(contexts[head, span, :128], 32, 1)
            right = pltpu.roll(contexts[head, span, 128:], 32, 1)
            context = jnp.where(lanes < 32, left, right)
        else:
            context = pltpu.roll(contexts[head, span, :128], 96, 1)
        context = context / denominator
        lse = top * score_scale + jnp.log(denominator)
        coarse = lse.astype(jnp.bfloat16).astype(jnp.float32)
        middle = (lse - coarse).astype(jnp.bfloat16).astype(jnp.float32)
        fine = lse - coarse - middle
        tail = jnp.where(lanes == HD, coarse, jnp.where(lanes == HD + 1, middle, fine))
        out_ref[span, head * 128 : head * 128 + 128] = jnp.where(
            lanes < HD, context, tail
        ).astype(jnp.bfloat16)


def combine(flag_ref, parts_ref, att_ref, lse_ref):
    count = parts_ref.shape[0]
    live = flag_ref[0] == 0
    for head in range(2):
        parts = [
            parts_ref[i, :, head * 128 : head * 128 + 128].astype(jnp.float32)
            for i in range(count)
        ]
        lses = [p[:, 96:97] + p[:, 97:98] + p[:, 98:99] for p in parts]
        peak = functools.reduce(jnp.maximum, lses)
        weights = [jnp.exp(v - peak) for v in lses]
        total = functools.reduce(jnp.add, weights)
        context = functools.reduce(jnp.add, [p * w for p, w in zip(parts, weights)])
        lanes = lane_ids(context.shape)
        whole = jnp.where(lanes < HD, context / total, peak + jnp.log(total))
        turned = jnp.where(live, jnp.transpose(whole, (1, 0)), 0.0)
        att_ref[head * HD : head * HD + HD, :] = turned[:HD].astype(jnp.bfloat16)
        lse_ref[head : head + 1, :] = turned[HD : HD + 1]


SMEM = pl.BlockSpec(memory_space=pltpu.SMEM)
VMEM = pl.BlockSpec(memory_space=pltpu.VMEM)


def project(core, gathered, weight, extra=None):
    depth = gathered.shape[1]
    columns = weight.shape[0]
    blocks = weight.shape[1] // (2 * depth)
    rows = gathered.shape[0] // blocks
    x_spec = pl.BlockSpec((rows, depth), lambda i, c: (i, 0))
    w_spec = pl.BlockSpec((columns, depth), lambda i, c: (0, 2 * i + c[0]))

    def fixed(shape):
        return pl.BlockSpec(shape, lambda i, c: (0,) * len(shape))

    if extra is None:
        return pl.pallas_call(
            half_projection,
            grid_spec=pltpu.PrefetchScalarGridSpec(
                num_scalar_prefetch=1,
                grid=(blocks,),
                in_specs=[x_spec, w_spec],
                out_specs=fixed((rows, columns)),
            ),
            out_shape=jax.ShapeDtypeStruct((rows, columns), jnp.float32),
        )(core, gathered, weight)
    first, cosine, sine, page_map = extra
    return pl.pallas_call(
        rest_projection,
        grid_spec=pltpu.PrefetchScalarGridSpec(
            num_scalar_prefetch=1,
            grid=(blocks,),
            in_specs=[
                x_spec,
                w_spec,
                fixed((rows, columns)),
                fixed((rows, 128)),
                fixed((rows, 128)),
                fixed((1, 384)),
            ],
            out_specs=[fixed((rows, 384)), fixed((rows + 16, 384))],
            scratch_shapes=[pltpu.VMEM((rows, 640), jnp.float32)],
        ),
        out_shape=[
            jax.ShapeDtypeStruct((rows, 384), jnp.bfloat16),
            jax.ShapeDtypeStruct((rows + 16, 384), jnp.bfloat16),
        ],
    )(core, gathered, weight, first, cosine, sine, page_map)


def body(stream_x, qkv_weight, short_lengths, cache_owner):
    planes, columns = lax.axis_size("z"), lax.axis_size("y")
    tok_count = stream_x.shape[0]
    plane, column = lax.axis_index("z"), lax.axis_index("y")
    core = lax.axis_index("c").astype(jnp.int32).reshape(1)
    plane_rows = tok_count * columns
    long_planes = planes * 11 // 16
    long_length = plane_rows * long_planes
    bounds = boundaries(short_lengths, long_length)
    pad_segment = short_lengths.shape[0] + 1

    ours = lax.all_gather(stream_x, "x", axis=0, tiled=True)
    theirs = lax.ppermute(ours, "c", [(0, 1), (1, 0)])

    first_row = plane * plane_rows + column * tok_count
    row_ids = first_row + jnp.arange(tok_count, dtype=jnp.int32)
    segment, seg_begin = locate(row_ids, bounds)
    position = (row_ids - seg_begin).astype(jnp.float32)
    half_dim = HD // 2
    inverse_freq = rope_base ** (-jnp.arange(half_dim, dtype=jnp.float32) / half_dim)
    angle = position[:, None] * inverse_freq[None, :]
    cosine = jnp.cos(angle)
    sine = jnp.sin(angle)
    blank = jnp.zeros((tok_count, 128 - HD), jnp.float32)
    cosine = jnp.concatenate([cosine, cosine, blank], axis=1)
    sine = jnp.concatenate([-sine, sine, blank], axis=1)

    pages = tok_count // CAP
    owners = planes * columns
    page_owner = cache_owner.reshape(pages, CAP)[:, 0]
    page_live = segment.reshape(pages, CAP)[:, 0] != pad_segment
    hit = (page_owner[:, None] == jnp.arange(owners, dtype=jnp.int32)[None, :]) & page_live[:, None]
    page_map = jnp.max(
        jnp.where(hit, jnp.arange(pages, dtype=jnp.int32)[:, None], -1), axis=0
    ).astype(jnp.float32)
    page_map = jnp.concatenate([page_map, jnp.zeros((384 - owners,), jnp.float32)])[None, :]

    weight = qkv_weight.T
    half = project(core, ours, weight)
    queries, key_values = project(1 - core, theirs, weight, (half, cosine, sine, page_map))

    rows_sent = tok_count + 16
    gathered = lax.all_gather(key_values, "z", axis=0, tiled=True)
    plane_queries = lax.all_gather(queries, "y", axis=0, tiled=True)
    plane_ids = plane * plane_rows + jnp.arange(plane_rows, dtype=jnp.int32)
    unused, plane_begin = locate(plane_ids, bounds)

    is_long = plane < long_planes
    low = jnp.where(is_long, 0, jnp.maximum(plane - 1, long_planes))
    masked_low = jnp.where(is_long, plane, low)
    info = jnp.stack([plane, column, low, masked_low]).astype(jnp.int32)

    plane_begin = plane_begin[:, None]
    gathered, plane_queries, plane_begin, info = lax.optimization_barrier(
        (gathered, plane_queries, plane_begin, info)
    )

    by_plane = gathered.reshape(planes, rows_sent, 384)
    table = lax.dynamic_slice_in_dim(
        by_plane[:, tok_count, :owners], plane * columns, columns, 1
    ).astype(jnp.int32)
    outbox = pl.pallas_call(
        select_pages,
        in_specs=[SMEM, VMEM],
        out_specs=VMEM,
        out_shape=jax.ShapeDtypeStruct((columns, planes, CAP, 384), jnp.bfloat16),
    )(table.reshape(-1), gathered.reshape(planes, rows_sent // CAP, CAP, 384))
    received = lax.all_to_all(
        outbox.reshape(columns, planes * CAP, 384), "y", split_axis=0, concat_axis=0, tiled=True
    )
    kv_cache = (
        received.reshape(columns, planes, CAP, 384)
        .transpose(1, 0, 2, 3)
        .reshape(planes * columns * CAP, 384)
    )

    slots = 2 * ((max(long_planes, 2) + 1) // 2)
    partial = pl.pallas_call(
        attention,
        in_specs=[SMEM, VMEM, VMEM, VMEM],
        out_specs=VMEM,
        out_shape=jax.ShapeDtypeStruct((plane_rows, 256), jnp.bfloat16),
        scratch_shapes=[
            pltpu.VMEM((slots, 2, plane_rows, 256), jnp.float32),
            pltpu.VMEM((2, plane_rows, 128), jnp.float32),
            pltpu.VMEM((2, plane_rows, 128), jnp.float32),
            pltpu.VMEM((2, plane_rows, 256), jnp.float32),
        ],
    )(info, plane_queries, plane_begin, by_plane)
    parts = lax.all_to_all(
        partial.reshape(columns, tok_count, 256), "y", split_axis=0, concat_axis=0, tiled=True
    )
    is_padding = (segment[:1] == pad_segment).astype(jnp.int32)
    attended, row_lse = pl.pallas_call(
        combine,
        in_specs=[SMEM, VMEM],
        out_specs=[VMEM, VMEM],
        out_shape=[
            jax.ShapeDtypeStruct((2 * HD, tok_count), jnp.bfloat16),
            jax.ShapeDtypeStruct((2, tok_count), jnp.float32),
        ],
    )(is_padding, parts)
    return (attended.T, row_lse, kv_cache)


def solution(mesh):
    seq, head = mesh.devices.shape
    fine = Mesh(mesh.devices.reshape(seq // 4, 4, head // 2, 2), ("z", "y", "x", "c"))
    seq_axes, head_axes = ("z", "y"), ("x", "c")
    return jax.shard_map(
        body,
        mesh=fine,
        in_specs=(P(seq_axes, head_axes), P(None, head_axes), P(), P(seq_axes, None)),
        out_specs=(P(seq_axes, head_axes), P(head_axes, seq_axes), P(seq_axes, head_axes)),
        check_vma=False,
    )
```

```python
import functools
import math

import jax
import jax.numpy as jnp
from jax import lax
from jax.experimental import pallas as pl
from jax.experimental.pallas import tpu as pltpu
from jax.sharding import Mesh, PartitionSpec as P

HD = 96
CAP = 8
neg_large = -1e30
rope_base = 10000.0
score_scale = 1.0 / math.sqrt(HD)
log2_scale = score_scale * math.log2(math.e)


def boundaries(short_lengths, long_length):
    count = short_lengths.shape[0]
    before = jnp.arange(count)[None, :] < jnp.arange(count + 1)[:, None]
    return jnp.sum(jnp.where(before, short_lengths[None, :], 0), axis=1) + long_length


PAIR = 2
KEYS = 256
MESH_Y = 4


def lane_ids(shape):
    return lax.broadcasted_iota(jnp.int32, shape, 1)


def block_sum(core, x_ref, w_ref):
    rows = 256
    depth = x_ref.shape[1]
    total = None
    for i in range(x_ref.shape[0] // rows):
        first = pl.multiple_of((2 * i + core) * depth, 128)
        part = lax.dot_general(
            x_ref[i * rows : (i + 1) * rows, :],
            w_ref[:, pl.ds(first, depth)],
            (((1,), (1,)), ((), ())),
            preferred_element_type=jnp.float32,
        )
        total = part if total is None else total + part
    return total


def half_projection(core_ref, x_ref, w_ref, out_ref):
    out_ref[...] = block_sum(core_ref[0], x_ref, w_ref)


def pack_heads(p0, p1, p2, p3):
    lanes = lane_ids(p0.shape)
    r1 = pltpu.roll(p1, 96, 1)
    r2 = pltpu.roll(p2, 64, 1)
    r3 = pltpu.roll(p3, 32, 1)
    return (
        jnp.where(lanes < 96, p0, r1),
        jnp.where(lanes < 64, r1, r2),
        jnp.where(lanes < 32, r2, r3),
    )


def rest_projection(core_ref, x_ref, w_ref, first_ref, cos_ref, sin_ref, q_ref, kv_ref):
    total = first_ref[...] + block_sum(core_ref[0], x_ref, w_ref)
    rows, columns = total.shape
    width = columns + 64
    whole = jnp.concatenate([total, jnp.zeros((rows, 64), jnp.float32)], axis=1)
    cosine = cos_ref[...]
    sine = sin_ref[...]
    lanes = lane_ids((rows, 128))

    def window(first):
        return pltpu.roll(whole, (width - first) % width, 1)[:, :128]

    def rotated(first):
        here = window(first)
        ahead = window(first + 48)
        behind = window((first - 48) % width)
        return here * cosine + jnp.where(lanes < 48, ahead, behind) * sine

    def plain(first):
        return jnp.where(lanes < HD, window(first), 0.0)

    key_values = pack_heads(rotated(96), plain(192), rotated(384), plain(480))
    for i in range(3):
        kv_ref[:, 128 * i : 128 * i + 128] = key_values[i].astype(jnp.bfloat16)
    q_ref[:, :128] = rotated(0).astype(jnp.bfloat16)
    q_ref[:, 128:] = rotated(288)[:, :HD].astype(jnp.bfloat16)


def attention(
    info_ref,
    table_ref,
    q_ref,
    ends_ref,
    kv_hbm,
    blank_ref,
    out_hbm,
    kv_ref,
    qs,
    scores,
    peaks,
    totals,
    contexts,
    outs,
    pages,
    kv_sems,
    page_sem,
    out_sem,
):
    group, member, column = info_ref[0], info_ref[1], info_ref[2]
    groups = kv_ref.shape[0]
    rows = MESH_Y * KEYS
    chunk = 256
    targets = outs.shape[0]
    long_planes = 11 * groups * PAIR // 16

    def fetch(k):
        return pltpu.make_async_copy(kv_hbm.at[k], kv_ref.at[k], kv_sems.at[k])

    least = jnp.where(group * PAIR < long_planes, 0, group - 1)

    def start_fetch(k, carry):
        fetch(k).start()
        return carry

    def wait_fetch(k, carry):
        fetch(k).wait()
        return carry

    lax.fori_loop(least, group + 1, start_fetch, 0)

    def send_page(i, carry):
        k = i // targets
        t = i % targets
        page = table_ref[i]
        there = pages.at[t, pl.ds(pl.multiple_of(k * CAP, CAP), CAP), :]

        @pl.when(page >= 0)
        def _():
            first = pl.multiple_of(jnp.maximum(page, 0) * CAP, CAP)
            pltpu.make_async_copy(kv_hbm.at[k, pl.ds(first, CAP), :], there, page_sem).start()

        @pl.when(page < 0)
        def _():
            pltpu.make_async_copy(blank_ref, there, page_sem).start()

        return carry

    lax.fori_loop(0, groups * targets, send_page, 0)

    key_cols = (slice(0, 128), slice(128, 384))
    value_cols = (slice(0, 256), slice(256, 384))
    value_width = (256, 128)
    parts = [
        (head, slice(first, first + chunk), first)
        for head in range(2)
        for first in range(0, rows, chunk)
    ]
    lanes = lane_ids((chunk, 128))

    def one_plane(h, waits):
        plane = group * PAIR + h
        is_long = plane < long_planes
        low = jnp.where(is_long, 0, group - 1)
        masked_low = jnp.where(is_long, group, group - 1)
        count = group + 1 - low

        for first in range(0, rows, chunk):
            start = h * rows + first
            if not isinstance(start, int):
                start = pl.multiple_of(start, chunk)
            here = pl.ds(start, chunk)
            q1 = q_ref[here, 128 : 128 + HD].astype(jnp.float32)
            q1 = jnp.concatenate([q1, jnp.zeros((chunk, 128 - HD), jnp.float32)], axis=1)
            q1 = pltpu.roll(q1, 64, 1)
            span = slice(first, first + chunk)
            qs[span, :128] = q_ref[here, :128]
            qs[span, 128:256] = jnp.where(lanes < 64, 0.0, q1).astype(jnp.bfloat16)
            qs[span, 256:] = jnp.where(lanes < 32, q1, 0.0).astype(jnp.bfloat16)

        peaks[...] = jnp.full_like(peaks, neg_large)
        totals[...] = jnp.zeros_like(totals)
        contexts[...] = jnp.zeros_like(contexts)

        if waits:
            lax.fori_loop(least, group + 1, wait_fetch, 0)

        def score(k, masked):
            for head, span, first in parts:
                s = lax.dot_general(
                    qs[span, key_cols[head]],
                    kv_ref[k, :, key_cols[head]],
                    (((1,), (1,)), ((), ())),
                    preferred_element_type=jnp.float32,
                )
                if masked:
                    shape = (chunk, KEYS)
                    row_ids = plane * rows + first + lax.broadcasted_iota(jnp.int32, shape, 0)
                    key_ids = (
                        (k * PAIR + member) * rows
                        + column * KEYS
                        + lax.broadcasted_iota(jnp.int32, shape, 1)
                    )
                    allowed = (key_ids <= row_ids) & (row_ids < ends_ref[pl.ds(k, 1), :])
                    s = jnp.where(allowed, s, neg_large)
                scores[k - low, head, span, :] = s
                peaks[head, span, :] = jnp.maximum(
                    peaks[head, span, :], jnp.maximum(s[:, :128], s[:, 128:])
                )

        def free_step(k, carry):
            score(k, False)
            return carry

        def masked_step(k, carry):
            score(k, True)
            return carry

        lax.fori_loop(low, masked_low, free_step, 0)
        lax.fori_loop(masked_low, group + 1, masked_step, 0)

        @pl.when(count % 2 == 1)
        def _():
            scores[count] = jnp.full(scores.shape[1:], neg_large, jnp.float32)

        tops = []
        for head, span, first in parts:
            top = jnp.max(peaks[head, span, :], axis=1, keepdims=True)
            tops.append(top)
            peaks[head, span, :] = jnp.broadcast_to(top * log2_scale, (chunk, 128))

        def weigh(i, carry):
            for head, span, first in parts:
                shift = peaks[head, span, :]
                total = totals[head, span, :]
                context = contexts[head, span, : value_width[head]]
                for n in range(2):
                    slot = 2 * i + n
                    k = jnp.minimum(low + slot, group)
                    s = scores[slot, head, span, :]
                    left = jnp.exp2(s[:, :128] * log2_scale - shift)
                    right = jnp.exp2(s[:, 128:] * log2_scale - shift)
                    total = total + (left + right)
                    p = jnp.concatenate(
                        [left.astype(jnp.bfloat16), right.astype(jnp.bfloat16)], axis=1
                    )
                    context = context + jnp.dot(
                        p, kv_ref[k, :, value_cols[head]], preferred_element_type=jnp.float32
                    )
                totals[head, span, :] = total
                contexts[head, span, : value_width[head]] = context
            return carry

        lax.fori_loop(0, (count + 1) // 2, weigh, 0)

        for (head, span, first), top in zip(parts, tops):
            denominator = jnp.sum(totals[head, span, :], axis=1, keepdims=True)
            if head == 0:
                left = pltpu.roll(contexts[head, span, :128], 32, 1)
                right = pltpu.roll(contexts[head, span, 128:], 32, 1)
                context = jnp.where(lanes < 32, left, right)
            else:
                context = pltpu.roll(contexts[head, span, :128], 96, 1)
            context = context / denominator
            lse = top * score_scale + jnp.log(denominator)
            coarse = lse.astype(jnp.bfloat16).astype(jnp.float32)
            middle = (lse - coarse).astype(jnp.bfloat16).astype(jnp.float32)
            fine = lse - coarse - middle
            tail = jnp.where(lanes == HD, coarse, jnp.where(lanes == HD + 1, middle, fine))
            outs[h * MESH_Y + first // KEYS, :, head * 128 : head * 128 + 128] = jnp.where(
                lanes < HD, context, tail
            ).astype(jnp.bfloat16)

    page_rows = groups * CAP
    for h in range(PAIR):
        one_plane(h, h == 0)

    pltpu.make_async_copy(pages, pages, page_sem).wait()
    sends = [
        pltpu.make_async_copy(pages, out_hbm.at[:, pl.ds(0, page_rows), :], page_sem),
        pltpu.make_async_copy(
            outs, out_hbm.at[:, pl.ds(page_rows, KEYS), pl.ds(0, 256)], out_sem
        ),
    ]
    for send in sends:
        send.start()
    for send in sends:
        send.wait()


def combine(
    flag_ref, pages_hbm, got_hbm, att_ref, lse_ref, cache_ref, parts_ref, pages_ref, parts_sem, pages_sem
):
    count = parts_ref.shape[0]
    groups = cache_ref.shape[0]
    load = pltpu.make_async_copy(
        got_hbm.at[:, pl.ds(groups * CAP, KEYS), pl.ds(0, 256)], parts_ref, parts_sem
    )
    load.start()
    load_pages = pltpu.make_async_copy(pages_hbm.at[:, pl.ds(0, groups)], pages_ref, pages_sem)
    load_pages.start()
    load.wait()
    live = flag_ref[0] == 0
    for head in range(2):
        parts = [
            parts_ref[i, :, head * 128 : head * 128 + 128].astype(jnp.float32)
            for i in range(count)
        ]
        lses = [p[:, 96:97] + p[:, 97:98] + p[:, 98:99] for p in parts]
        peak = functools.reduce(jnp.maximum, lses)
        weights = [jnp.exp(v - peak) for v in lses]
        total = functools.reduce(jnp.add, weights)
        context = functools.reduce(jnp.add, [p * w for p, w in zip(parts, weights)])
        lanes = lane_ids(context.shape)
        whole = jnp.where(lanes < HD, context / total, peak + jnp.log(total))
        turned = jnp.where(live, jnp.transpose(whole, (1, 0)), 0.0)
        att_ref[head * HD : head * HD + HD, :] = turned[:HD].astype(jnp.bfloat16)
        lse_ref[head : head + 1, :] = turned[HD : HD + 1]
    load_pages.wait()
    for t in range(count):
        cache_ref[:, t] = pages_ref[t]


SMEM = pl.BlockSpec(memory_space=pltpu.SMEM)
VMEM = pl.BlockSpec(memory_space=pltpu.VMEM)
ANY = pl.BlockSpec(memory_space=pl.ANY)
SMALL = pltpu.CompilerParams(vmem_limit_bytes=40 << 20)


def in_vmem(x):
    return pltpu.with_memory_space_constraint(x, pltpu.VMEM)


def in_hbm(x):
    return pltpu.with_memory_space_constraint(x, pltpu.HBM)


def body(stream_x, qkv_weight, short_lengths, cache_owner):
    groups, columns = lax.axis_size("q"), lax.axis_size("y")
    targets = PAIR * columns
    tok_count = stream_x.shape[0]
    group, member, column = lax.axis_index("q"), lax.axis_index("p"), lax.axis_index("y")
    plane = group * PAIR + member
    core = lax.axis_index("c").astype(jnp.int32).reshape(1)
    plane_rows = tok_count * columns
    long_planes = groups * PAIR * 11 // 16
    bounds = boundaries(short_lengths, plane_rows * long_planes)

    weight = in_vmem(qkv_weight.T)
    ours = lax.all_gather(stream_x, "x", axis=0, tiled=True)
    theirs = lax.ppermute(ours, "c", [(0, 1), (1, 0)])

    row_ids = (
        plane * plane_rows + column * tok_count + jnp.arange(tok_count, dtype=jnp.int32)
    )
    passed = row_ids[:, None] >= bounds[None, :]
    seg_begin = jnp.max(jnp.where(passed, bounds[None, :], 0), axis=1)
    position = (row_ids - seg_begin).astype(jnp.float32)
    half_dim = HD // 2
    lane = jnp.arange(128, dtype=jnp.int32)
    entry = jnp.where(lane < half_dim, lane, lane - half_dim)
    inverse_freq = rope_base ** (-entry.astype(jnp.float32) / half_dim)
    sign = jnp.where(lane < half_dim, -1.0, jnp.where(lane < HD, 1.0, 0.0))
    angle = position[:, None] * inverse_freq[None, :]
    cosine = jnp.where(lane[None, :] < HD, jnp.cos(angle), 0.0)
    sine = jnp.sin(angle) * sign[None, :]

    half = pl.pallas_call(
        half_projection,
        in_specs=[SMEM, VMEM, VMEM],
        out_specs=VMEM,
        out_shape=jax.ShapeDtypeStruct((tok_count, qkv_weight.shape[1]), jnp.float32),
        compiler_params=SMALL,
    )(core, in_vmem(ours), weight)
    queries, key_values = pl.pallas_call(
        rest_projection,
        in_specs=[SMEM] + [VMEM] * 5,
        out_specs=[VMEM, VMEM],
        out_shape=[
            jax.ShapeDtypeStruct((tok_count, 128 + HD), jnp.bfloat16),
            jax.ShapeDtypeStruct((tok_count, 384), jnp.bfloat16),
        ],
        compiler_params=SMALL,
    )(1 - core, in_vmem(theirs), weight, in_vmem(half), in_vmem(cosine), in_vmem(sine))

    gathered = lax.all_gather(key_values, "q", axis=0, tiled=True)
    queries, short_lengths, cache_owner = lax.optimization_barrier(
        (queries, short_lengths, cache_owner)
    )
    plane_queries = lax.all_gather(queries, ("p", "y"), axis=0, tiled=True)

    bounds = boundaries(short_lengths, plane_rows * long_planes)
    key_ids = (
        (jnp.arange(groups, dtype=jnp.int32) * PAIR + member) * plane_rows + column * tok_count
    )[:, None] + jnp.arange(tok_count, dtype=jnp.int32)[None, :]
    ends = jnp.min(
        jnp.where(bounds[None, None, :] > key_ids[:, :, None], bounds[None, None, :], 1 << 30),
        axis=2,
    )

    pages = tok_count // CAP
    owners = groups * PAIR * columns
    page_owner = cache_owner.reshape(pages, CAP)[:, 0]
    page_live = row_ids.reshape(pages, CAP)[:, 0] < bounds[-1]
    hit = (page_owner[:, None] == jnp.arange(owners, dtype=jnp.int32)[None, :]) & page_live[:, None]
    page_map = jnp.max(jnp.where(hit, jnp.arange(pages, dtype=jnp.int32)[:, None], -1), axis=0)
    maps = lax.all_gather(page_map[None, :], "q", axis=0, tiled=True)
    table = lax.dynamic_slice_in_dim(maps, group * targets, targets, 1).reshape(-1)
    info = jnp.stack([group, member, column]).astype(jnp.int32)
    blank = jnp.zeros((CAP, 384), jnp.bfloat16)
    gathered, plane_queries, ends, table, info, blank = lax.optimization_barrier(
        (gathered, plane_queries, ends, table, info, blank)
    )

    most = max((long_planes - 1) // PAIR + 1, 2)
    slots = 2 * ((most + 1) // 2)
    page_rows = groups * CAP
    outbox = pl.pallas_call(
        attention,
        in_specs=[SMEM, SMEM, VMEM, VMEM, ANY, VMEM],
        out_specs=ANY,
        out_shape=jax.ShapeDtypeStruct((targets, page_rows + tok_count, 384), jnp.bfloat16),
        scratch_shapes=[
            pltpu.VMEM((groups, tok_count, 384), jnp.bfloat16),
            pltpu.VMEM((plane_rows, 384), jnp.bfloat16),
            pltpu.VMEM((slots, 2, plane_rows, 256), jnp.float32),
            pltpu.VMEM((2, plane_rows, 128), jnp.float32),
            pltpu.VMEM((2, plane_rows, 128), jnp.float32),
            pltpu.VMEM((2, plane_rows, 256), jnp.float32),
            pltpu.VMEM((targets, tok_count, 256), jnp.bfloat16),
            pltpu.VMEM((targets, page_rows, 384), jnp.bfloat16),
            pltpu.SemaphoreType.DMA((groups,)),
            pltpu.SemaphoreType.DMA,
            pltpu.SemaphoreType.DMA,
        ],
    )(info, table, plane_queries, ends, gathered.reshape(groups, tok_count, 384), blank)
    received = lax.all_to_all(outbox, ("p", "y"), split_axis=0, concat_axis=0, tiled=True)
    padding = (row_ids[:1] >= bounds[-1]).astype(jnp.int32)
    attended, row_lse, kv_cache = pl.pallas_call(
        combine,
        in_specs=[SMEM, ANY, ANY],
        out_specs=[VMEM, VMEM, VMEM],
        out_shape=[
            jax.ShapeDtypeStruct((2 * HD, tok_count), jnp.bfloat16),
            jax.ShapeDtypeStruct((2, tok_count), jnp.float32),
            jax.ShapeDtypeStruct((groups, targets, CAP, 384), jnp.bfloat16),
        ],
        scratch_shapes=[
            pltpu.VMEM((targets, tok_count, 256), jnp.bfloat16),
            pltpu.VMEM((targets, groups, CAP, 384), jnp.bfloat16),
            pltpu.SemaphoreType.DMA,
            pltpu.SemaphoreType.DMA,
        ],
    )(
        padding,
        received.reshape(targets, (page_rows + tok_count) // CAP, CAP, 384),
        received,
    )
    return (attended.T, row_lse, kv_cache.reshape(-1, 384))


def solution(mesh):
    seq, head = mesh.devices.shape
    shape = (seq // (MESH_Y * PAIR), PAIR, MESH_Y, head // 2, 2)
    fine = Mesh(mesh.devices.reshape(shape), ("q", "p", "y", "x", "c"))
    seq_axes, head_axes = ("q", "p", "y"), ("x", "c")
    return jax.shard_map(
        body,
        mesh=fine,
        in_specs=(P(seq_axes, head_axes), P(None, head_axes), P(), P(seq_axes, None)),
        out_specs=(P(seq_axes, head_axes), P(head_axes, seq_axes), P(seq_axes, head_axes)),
        check_vma=False,
    )
```

```python
import functools
import math

import jax
import jax.numpy as jnp
from jax import lax
from jax.experimental import pallas as pl
from jax.experimental.pallas import tpu as pltpu
from jax.sharding import Mesh, PartitionSpec as P

HD = 96
CAP = 8
neg_large = -1e30
rope_base = 10000.0
score_scale = 1.0 / math.sqrt(HD)
log2_scale = score_scale * math.log2(math.e)


def boundaries(short_lengths, long_length):
    count = short_lengths.shape[0]
    before = jnp.arange(count)[None, :] < jnp.arange(count + 1)[:, None]
    return jnp.sum(jnp.where(before, short_lengths[None, :], 0), axis=1) + long_length


PAIR = 2
KEYS = 256
MESH_Y = 4


def lane_ids(shape):
    return lax.broadcasted_iota(jnp.int32, shape, 1)


def block_sum(core, x_ref, w_ref):
    rows = 256
    depth = x_ref.shape[1]
    total = None
    for i in range(x_ref.shape[0] // rows):
        first = pl.multiple_of((2 * i + core) * depth, 128)
        part = lax.dot_general(
            x_ref[i * rows : (i + 1) * rows, :],
            w_ref[:, pl.ds(first, depth)],
            (((1,), (1,)), ((), ())),
            preferred_element_type=jnp.float32,
        )
        total = part if total is None else total + part
    return total


def half_projection(core_ref, x_ref, w_ref, out_ref):
    out_ref[...] = block_sum(core_ref[0], x_ref, w_ref)


def pack_heads(p0, p1, p2, p3):
    lanes = lane_ids(p0.shape)
    r1 = pltpu.roll(p1, 96, 1)
    r2 = pltpu.roll(p2, 64, 1)
    r3 = pltpu.roll(p3, 32, 1)
    return (
        jnp.where(lanes < 96, p0, r1),
        jnp.where(lanes < 64, r1, r2),
        jnp.where(lanes < 32, r2, r3),
    )


def rest_projection(
    core_ref, x_ref, w_ref, first_ref, cos_ref, sin_ref, owner_ref, q_ref, kv_ref
):
    total = first_ref[...] + block_sum(core_ref[0], x_ref, w_ref)
    rows, columns = total.shape
    width = columns + 64
    whole = jnp.concatenate([total, jnp.zeros((rows, 64), jnp.float32)], axis=1)
    cosine = cos_ref[...]
    sine = sin_ref[...]
    lanes = lane_ids((rows, 128))

    def window(first):
        return pltpu.roll(whole, (width - first) % width, 1)[:, :128]

    def rotated(first):
        here = window(first)
        ahead = window(first + 48)
        behind = window((first - 48) % width)
        return here * cosine + jnp.where(lanes < 48, ahead, behind) * sine

    def plain(first):
        return jnp.where(lanes < HD, window(first), 0.0)

    key_values = pack_heads(rotated(96), plain(192), rotated(384), plain(480))
    for i in range(3):
        kv_ref[:rows, 128 * i : 128 * i + 128] = key_values[i].astype(jnp.bfloat16)
    extra = kv_ref.shape[0] - rows
    kv_ref[rows:, :rows] = jnp.broadcast_to(owner_ref[...], (extra, rows)).astype(jnp.bfloat16)
    kv_ref[rows:, rows:] = jnp.zeros((extra, 384 - rows), jnp.bfloat16)
    q_ref[:, :128] = rotated(0).astype(jnp.bfloat16)
    q_ref[:, 128:] = rotated(288)[:, :HD].astype(jnp.bfloat16)


def attention(
    info_ref, q_ref, ends_ref, kv_hbm, out_ref, kv_ref, qs, scores, peaks, totals, contexts, kv_sems
):
    group, member, column = info_ref[0], info_ref[1], info_ref[2]
    groups = kv_ref.shape[0]
    rows = MESH_Y * KEYS
    chunk = 256
    targets = out_ref.shape[0]
    page_rows = groups * CAP
    long_planes = 11 * groups * PAIR // 16

    def fetch(k):
        return pltpu.make_async_copy(kv_hbm.at[k], kv_ref.at[k], kv_sems.at[k])

    least = jnp.where(group * PAIR < long_planes, 0, group - 1)

    def start_fetch(k, carry):
        fetch(k).start()
        return carry

    def wait_fetch(k, carry):
        fetch(k).wait()
        return carry

    lax.fori_loop(least, group + 1, start_fetch, 0)
    lax.fori_loop(0, least, start_fetch, 0)
    lax.fori_loop(group + 1, groups, start_fetch, 0)

    key_cols = (slice(0, 128), slice(128, 384))
    value_cols = (slice(0, 256), slice(256, 384))
    value_width = (256, 128)
    parts = [
        (head, slice(first, first + chunk), first)
        for head in range(2)
        for first in range(0, rows, chunk)
    ]
    lanes = lane_ids((chunk, 128))

    def one_plane(h, waits):
        plane = group * PAIR + h
        is_long = plane < long_planes
        low = jnp.where(is_long, 0, group - 1)
        masked_low = jnp.where(is_long, group, group - 1)
        count = group + 1 - low

        for first in range(0, rows, chunk):
            start = h * rows + first
            if not isinstance(start, int):
                start = pl.multiple_of(start, chunk)
            here = pl.ds(start, chunk)
            q1 = q_ref[here, 128 : 128 + HD].astype(jnp.float32)
            q1 = jnp.concatenate([q1, jnp.zeros((chunk, 128 - HD), jnp.float32)], axis=1)
            q1 = pltpu.roll(q1, 64, 1)
            span = slice(first, first + chunk)
            qs[span, :128] = q_ref[here, :128]
            qs[span, 128:256] = jnp.where(lanes < 64, 0.0, q1).astype(jnp.bfloat16)
            qs[span, 256:] = jnp.where(lanes < 32, q1, 0.0).astype(jnp.bfloat16)

        peaks[...] = jnp.full_like(peaks, neg_large)
        totals[...] = jnp.zeros_like(totals)
        contexts[...] = jnp.zeros_like(contexts)

        if waits:
            lax.fori_loop(least, group + 1, wait_fetch, 0)

        def score(k, masked):
            for head, span, first in parts:
                s = lax.dot_general(
                    qs[span, key_cols[head]],
                    kv_ref[k, :KEYS, key_cols[head]],
                    (((1,), (1,)), ((), ())),
                    preferred_element_type=jnp.float32,
                )
                if masked:
                    shape = (chunk, KEYS)
                    row_ids = plane * rows + first + lax.broadcasted_iota(jnp.int32, shape, 0)
                    key_ids = (
                        (k * PAIR + member) * rows
                        + column * KEYS
                        + lax.broadcasted_iota(jnp.int32, shape, 1)
                    )
                    allowed = (key_ids <= row_ids) & (row_ids < ends_ref[pl.ds(k, 1), :])
                    s = jnp.where(allowed, s, neg_large)
                scores[k - low, head, span, :] = s
                peaks[head, span, :] = jnp.maximum(
                    peaks[head, span, :], jnp.maximum(s[:, :128], s[:, 128:])
                )

        def free_step(k, carry):
            score(k, False)
            return carry

        def masked_step(k, carry):
            score(k, True)
            return carry

        lax.fori_loop(low, masked_low, free_step, 0)
        lax.fori_loop(masked_low, group + 1, masked_step, 0)

        @pl.when(count % 2 == 1)
        def _():
            scores[count] = jnp.full(scores.shape[1:], neg_large, jnp.float32)

        tops = []
        for head, span, first in parts:
            top = jnp.max(peaks[head, span, :], axis=1, keepdims=True)
            tops.append(top)
            peaks[head, span, :] = jnp.broadcast_to(top * log2_scale, (chunk, 128))

        def weigh(i, carry):
            for head, span, first in parts:
                shift = peaks[head, span, :]
                total = totals[head, span, :]
                context = contexts[head, span, : value_width[head]]
                for n in range(2):
                    slot = 2 * i + n
                    k = jnp.minimum(low + slot, group)
                    s = scores[slot, head, span, :]
                    left = jnp.exp2(s[:, :128] * log2_scale - shift)
                    right = jnp.exp2(s[:, 128:] * log2_scale - shift)
                    total = total + (left + right)
                    p = jnp.concatenate(
                        [left.astype(jnp.bfloat16), right.astype(jnp.bfloat16)], axis=1
                    )
                    context = context + jnp.dot(
                        p, kv_ref[k, :KEYS, value_cols[head]], preferred_element_type=jnp.float32
                    )
                totals[head, span, :] = total
                contexts[head, span, : value_width[head]] = context
            return carry

        lax.fori_loop(0, (count + 1) // 2, weigh, 0)

        for first in range(0, rows, chunk):
            span = slice(first, first + chunk)
            found = []
            columns = []
            for head in range(2):
                top = tops[head * (rows // chunk) + first // chunk]
                denominator = jnp.sum(totals[head, span, :], axis=1, keepdims=True)
                if head == 0:
                    left = pltpu.roll(contexts[head, span, :128], 32, 1)
                    right = pltpu.roll(contexts[head, span, 128:], 32, 1)
                    context = jnp.where(lanes < 32, left, right)
                else:
                    context = pltpu.roll(contexts[head, span, :128], 96, 1)
                found.append(jnp.where(lanes < HD, context / denominator, 0.0))
                lse = top * score_scale + jnp.log(denominator)
                coarse = lse.astype(jnp.bfloat16).astype(jnp.float32)
                middle = (lse - coarse).astype(jnp.bfloat16).astype(jnp.float32)
                columns += [coarse, middle, lse - coarse - middle]
            target = h * MESH_Y + first // KEYS
            mid = chunk // 2
            packed = pack_heads(found[0][:mid], found[1][:mid], found[0][mid:], found[1][mid:])
            for i in range(3):
                out_ref[target, page_rows : page_rows + mid, 128 * i : 128 * i + 128] = packed[
                    i
                ].astype(jnp.bfloat16)
            spread = jnp.zeros((chunk, 128), jnp.float32)
            for i, value in enumerate(columns):
                spread = jnp.where(lanes == i, value, spread)
            tail = slice(page_rows + mid, page_rows + mid + 16)
            out_ref[target, tail, :chunk] = jnp.transpose(spread, (1, 0))[:16].astype(jnp.bfloat16)
            out_ref[target, tail, chunk:] = jnp.zeros((16, 384 - chunk), jnp.bfloat16)

    for h in range(PAIR):
        one_plane(h, h == 0)

    lax.fori_loop(0, least, wait_fetch, 0)
    lax.fori_loop(group + 1, groups, wait_fetch, 0)
    shape = (targets * 16, KEYS)
    row = lax.broadcasted_iota(jnp.int32, shape, 0)
    key = lax.broadcasted_iota(jnp.int32, shape, 1)
    same_place = (row & 7) == (key & 7)
    parity = (row >> 3) & 1
    owner = (group * targets + (row >> 4)).astype(jnp.float32)
    for two in range(groups // 2):
        total = None
        for n in range(2):
            k = 2 * two + n
            owners = kv_ref[k, KEYS : KEYS + 16, :KEYS].astype(jnp.float32)[:1]
            chosen = (owners == owner) & same_place & (parity == n)
            picked = jnp.dot(
                jnp.where(chosen, 1.0, 0.0).astype(jnp.bfloat16),
                kv_ref[k, :KEYS, :],
                preferred_element_type=jnp.float32,
            )
            total = picked if total is None else total + picked
        total = total.astype(jnp.bfloat16)
        for t in range(targets):
            out_ref[t, 16 * two : 16 * two + 16, :] = total[16 * t : 16 * t + 16]


def combine(
    flag_ref, pages_hbm, got_hbm, att_ref, lse_ref, cache_ref, parts_ref, pages_ref, parts_sem, pages_sem
):
    count = parts_ref.shape[0]
    groups = cache_ref.shape[0]
    load = pltpu.make_async_copy(
        got_hbm.at[:, pl.ds(groups * CAP, parts_ref.shape[1]), :], parts_ref, parts_sem
    )
    load.start()
    load_pages = pltpu.make_async_copy(pages_hbm.at[:, pl.ds(0, groups)], pages_ref, pages_sem)
    load_pages.start()
    load.wait()
    live = flag_ref[0] == 0
    mid = KEYS // 2
    shares = []
    for head in range(2):
        lses = []
        for i in range(count):
            rows = parts_ref[i, mid : mid + 16, :KEYS].astype(jnp.float32)
            first = 3 * head
            lses.append(
                rows[first : first + 1] + rows[first + 1 : first + 2] + rows[first + 2 : first + 3]
            )
        lses = jnp.concatenate(lses, axis=0)
        peak = jnp.max(lses, axis=0, keepdims=True)
        weights = jnp.exp(lses - peak)
        total = jnp.sum(weights, axis=0, keepdims=True)
        shares.append(weights / total)
        lse_ref[head : head + 1, :] = jnp.where(live, peak + jnp.log(total), 0.0)
    shares.append(jnp.zeros((128 - 2 * count, KEYS), jnp.float32))
    shares = jnp.transpose(jnp.concatenate(shares, axis=0), (1, 0))
    lanes = lane_ids((mid, 128))
    sums = [None] * 3
    for i in range(count):
        near0, near1 = shares[:mid, i : i + 1], shares[:mid, count + i : count + i + 1]
        far0, far1 = shares[mid:, i : i + 1], shares[mid:, count + i : count + i + 1]
        spread = (
            jnp.where(lanes < 96, near0, near1),
            jnp.where(lanes < 64, near1, far0),
            jnp.where(lanes < 32, far0, far1),
        )
        for j in range(3):
            part = parts_ref[i, :mid, 128 * j : 128 * j + 128].astype(jnp.float32) * spread[j]
            sums[j] = part if sums[j] is None else sums[j] + part
    turned = [
        jnp.where(live, jnp.transpose(v, (1, 0)), 0.0).astype(jnp.bfloat16) for v in sums
    ]
    att_ref[:128, :mid] = turned[0]
    att_ref[128:, :mid] = turned[1][:64]
    att_ref[:64, mid:] = turned[1][64:]
    att_ref[64:, mid:] = turned[2]
    load_pages.wait()
    for t in range(count):
        cache_ref[:, t] = pages_ref[t]


SMEM = pl.BlockSpec(memory_space=pltpu.SMEM)
VMEM = pl.BlockSpec(memory_space=pltpu.VMEM)
ANY = pl.BlockSpec(memory_space=pl.ANY)
SMALL = pltpu.CompilerParams(vmem_limit_bytes=40 << 20)


def in_vmem(x):
    return pltpu.with_memory_space_constraint(x, pltpu.VMEM)


def in_hbm(x):
    return pltpu.with_memory_space_constraint(x, pltpu.HBM)


def body(stream_x, qkv_weight, short_lengths, cache_owner):
    groups, columns = lax.axis_size("q"), lax.axis_size("y")
    targets = PAIR * columns
    tok_count = stream_x.shape[0]
    group, member, column = lax.axis_index("q"), lax.axis_index("p"), lax.axis_index("y")
    plane = group * PAIR + member
    core = lax.axis_index("c").astype(jnp.int32).reshape(1)
    plane_rows = tok_count * columns
    long_planes = groups * PAIR * 11 // 16
    bounds = boundaries(short_lengths, plane_rows * long_planes)

    weight = in_vmem(qkv_weight.T)
    ours = lax.all_gather(stream_x, "x", axis=0, tiled=True)
    theirs = lax.ppermute(ours, "c", [(0, 1), (1, 0)])

    row_ids = (
        plane * plane_rows + column * tok_count + jnp.arange(tok_count, dtype=jnp.int32)
    )
    passed = row_ids[:, None] >= bounds[None, :]
    seg_begin = jnp.max(jnp.where(passed, bounds[None, :], 0), axis=1)
    position = (row_ids - seg_begin).astype(jnp.float32)
    half_dim = HD // 2
    lane = jnp.arange(128, dtype=jnp.int32)
    entry = jnp.where(lane < half_dim, lane, lane - half_dim)
    inverse_freq = rope_base ** (-entry.astype(jnp.float32) / half_dim)
    sign = jnp.where(lane < half_dim, -1.0, jnp.where(lane < HD, 1.0, 0.0))
    angle = position[:, None] * inverse_freq[None, :]
    cosine = jnp.where(lane[None, :] < HD, jnp.cos(angle), 0.0)
    sine = jnp.sin(angle) * sign[None, :]

    owner_row = jnp.where(row_ids < bounds[-1], cache_owner.reshape(tok_count), -1)
    owner_row = owner_row.astype(jnp.float32)[None, :]

    half = pl.pallas_call(
        half_projection,
        in_specs=[SMEM, VMEM, VMEM],
        out_specs=VMEM,
        out_shape=jax.ShapeDtypeStruct((tok_count, qkv_weight.shape[1]), jnp.float32),
        compiler_params=SMALL,
    )(core, in_vmem(ours), weight)
    queries, key_values = pl.pallas_call(
        rest_projection,
        in_specs=[SMEM] + [VMEM] * 6,
        out_specs=[VMEM, VMEM],
        out_shape=[
            jax.ShapeDtypeStruct((tok_count, 128 + HD), jnp.bfloat16),
            jax.ShapeDtypeStruct((tok_count + 16, 384), jnp.bfloat16),
        ],
        compiler_params=SMALL,
    )(1 - core, in_vmem(theirs), weight, in_vmem(half), in_vmem(cosine), in_vmem(sine), owner_row)

    gathered = lax.all_gather(key_values, "q", axis=0, tiled=True)
    queries, short_lengths = lax.optimization_barrier((queries, short_lengths))
    plane_queries = lax.all_gather(queries, ("p", "y"), axis=0, tiled=True)

    bounds = boundaries(short_lengths, plane_rows * long_planes)
    key_ids = (
        (jnp.arange(groups, dtype=jnp.int32) * PAIR + member) * plane_rows + column * tok_count
    )[:, None] + jnp.arange(tok_count, dtype=jnp.int32)[None, :]
    ends = jnp.min(
        jnp.where(bounds[None, None, :] > key_ids[:, :, None], bounds[None, None, :], 1 << 30),
        axis=2,
    )

    info = jnp.stack([group, member, column]).astype(jnp.int32)
    gathered, plane_queries, ends, info = lax.optimization_barrier(
        (gathered, plane_queries, ends, info)
    )

    most = max((long_planes - 1) // PAIR + 1, 2)
    slots = 2 * ((most + 1) // 2)
    page_rows = groups * CAP
    box_rows = page_rows + tok_count // 2 + 16
    outbox = pl.pallas_call(
        attention,
        in_specs=[SMEM, VMEM, VMEM, ANY],
        out_specs=VMEM,
        out_shape=jax.ShapeDtypeStruct((targets, box_rows, 384), jnp.bfloat16),
        scratch_shapes=[
            pltpu.VMEM((groups, tok_count + 16, 384), jnp.bfloat16),
            pltpu.VMEM((plane_rows, 384), jnp.bfloat16),
            pltpu.VMEM((slots, 2, plane_rows, 256), jnp.float32),
            pltpu.VMEM((2, plane_rows, 128), jnp.float32),
            pltpu.VMEM((2, plane_rows, 128), jnp.float32),
            pltpu.VMEM((2, plane_rows, 256), jnp.float32),
            pltpu.SemaphoreType.DMA((groups,)),
        ],
    )(info, plane_queries, ends, gathered.reshape(groups, tok_count + 16, 384))
    received = lax.all_to_all(outbox, ("p", "y"), split_axis=0, concat_axis=0, tiled=True)
    padding = (row_ids[:1] >= bounds[-1]).astype(jnp.int32)
    attended, row_lse, kv_cache = pl.pallas_call(
        combine,
        in_specs=[SMEM, ANY, ANY],
        out_specs=[VMEM, VMEM, VMEM],
        out_shape=[
            jax.ShapeDtypeStruct((2 * HD, tok_count), jnp.bfloat16),
            jax.ShapeDtypeStruct((2, tok_count), jnp.float32),
            jax.ShapeDtypeStruct((groups, targets, CAP, 384), jnp.bfloat16),
        ],
        scratch_shapes=[
            pltpu.VMEM((targets, tok_count // 2 + 16, 384), jnp.bfloat16),
            pltpu.VMEM((targets, groups, CAP, 384), jnp.bfloat16),
            pltpu.SemaphoreType.DMA,
            pltpu.SemaphoreType.DMA,
        ],
    )(
        padding,
        received.reshape(targets, box_rows // CAP, CAP, 384),
        received,
    )
    return (attended.T, row_lse, kv_cache.reshape(-1, 384))


def solution(mesh):
    seq, head = mesh.devices.shape
    shape = (seq // (MESH_Y * PAIR), PAIR, MESH_Y, head // 2, 2)
    fine = Mesh(mesh.devices.reshape(shape), ("q", "p", "y", "x", "c"))
    seq_axes, head_axes = ("q", "p", "y"), ("x", "c")
    return jax.shard_map(
        body,
        mesh=fine,
        in_specs=(P(seq_axes, head_axes), P(None, head_axes), P(), P(seq_axes, None)),
        out_specs=(P(seq_axes, head_axes), P(head_axes, seq_axes), P(seq_axes, head_axes)),
        check_vma=False,
    )
```

```python
import functools
import math

import jax
import jax.numpy as jnp
from jax import lax
from jax.experimental import pallas as pl
from jax.experimental.pallas import tpu as pltpu
from jax.sharding import Mesh, PartitionSpec as P

HD = 96
CAP = 8
neg_large = -1e30
rope_base = 10000.0
score_scale = 1.0 / math.sqrt(HD)
log2_scale = score_scale * math.log2(math.e)


def boundaries(short_lengths, long_length):
    count = short_lengths.shape[0]
    before = jnp.arange(count)[None, :] < jnp.arange(count + 1)[:, None]
    return jnp.sum(jnp.where(before, short_lengths[None, :], 0), axis=1) + long_length


PAIR = 2
KEYS = 256
MESH_Y = 4


def lane_ids(shape):
    return lax.broadcasted_iota(jnp.int32, shape, 1)


def block_sum(core, x_ref, w_ref):
    rows = 256
    depth = x_ref.shape[1]
    total = None
    for i in range(x_ref.shape[0] // rows):
        first = pl.multiple_of((2 * i + core) * depth, 128)
        part = lax.dot_general(
            x_ref[i * rows : (i + 1) * rows, :],
            w_ref[:, pl.ds(first, depth)],
            (((1,), (1,)), ((), ())),
            preferred_element_type=jnp.float32,
        )
        total = part if total is None else total + part
    return total


def half_projection(core_ref, x_ref, w_ref, out_ref):
    out_ref[...] = block_sum(core_ref[0], x_ref, w_ref)


def pack_heads(p0, p1, p2, p3):
    lanes = lane_ids(p0.shape)
    r1 = pltpu.roll(p1, 96, 1)
    r2 = pltpu.roll(p2, 64, 1)
    r3 = pltpu.roll(p3, 32, 1)
    return (
        jnp.where(lanes < 96, p0, r1),
        jnp.where(lanes < 64, r1, r2),
        jnp.where(lanes < 32, r2, r3),
    )


def rest_projection(
    core_ref, x_ref, w_ref, first_ref, cos_ref, sin_ref, owner_ref, q_ref, kva_ref, kvb_ref
):
    total = first_ref[...] + block_sum(core_ref[0], x_ref, w_ref)
    rows, columns = total.shape
    width = columns + 64
    whole = jnp.concatenate([total, jnp.zeros((rows, 64), jnp.float32)], axis=1)
    cosine = cos_ref[...]
    sine = sin_ref[...]
    lanes = lane_ids((rows, 128))

    def window(first):
        return pltpu.roll(whole, (width - first) % width, 1)[:, :128]

    def rotated(first):
        here = window(first)
        ahead = window(first + 48)
        behind = window((first - 48) % width)
        return here * cosine + jnp.where(lanes < 48, ahead, behind) * sine

    def plain(first):
        return jnp.where(lanes < HD, window(first), 0.0)

    key_values = pack_heads(rotated(96), plain(192), rotated(384), plain(480))
    early = kva_ref.shape[0]
    for i in range(3):
        part = key_values[i].astype(jnp.bfloat16)
        kva_ref[:, 128 * i : 128 * i + 128] = part[:early]
        kvb_ref[: rows - early, 128 * i : 128 * i + 128] = part[early:]
    kvb_ref[rows - early :, :rows] = jnp.broadcast_to(owner_ref[...], (16, rows)).astype(
        jnp.bfloat16
    )
    kvb_ref[rows - early :, rows:] = jnp.zeros((16, 384 - rows), jnp.bfloat16)
    q_ref[:, :128] = rotated(0).astype(jnp.bfloat16)
    q_ref[:, 128:] = rotated(288)[:, :HD].astype(jnp.bfloat16)


def attention(
    info_ref,
    own_ref,
    other_ref,
    ends_ref,
    kva_hbm,
    kvb_hbm,
    out_ref,
    kv_ref,
    qs,
    scores,
    peaks,
    totals,
    contexts,
    kv_sems,
):
    group, member, column = info_ref[0], info_ref[1], info_ref[2]
    groups = kv_ref.shape[0]
    rows = MESH_Y * KEYS
    chunk = 256
    targets = out_ref.shape[0]
    page_rows = groups * CAP
    long_planes = 11 * groups * PAIR // 16

    early = kva_hbm.shape[1]

    def fetches(k):
        return (
            pltpu.make_async_copy(
                kva_hbm.at[k], kv_ref.at[k, pl.ds(0, early), :], kv_sems.at[k, 0]
            ),
            pltpu.make_async_copy(
                kvb_hbm.at[k], kv_ref.at[k, pl.ds(early, kvb_hbm.shape[1]), :], kv_sems.at[k, 1]
            ),
        )

    least = jnp.where(group * PAIR < long_planes, 0, group - 1)

    def start_fetch(k, carry):
        for copy in fetches(k):
            copy.start()
        return carry

    def wait_fetch(k, carry):
        for copy in fetches(k):
            copy.wait()
        return carry

    lax.fori_loop(least, group + 1, start_fetch, 0)
    lax.fori_loop(0, least, start_fetch, 0)
    lax.fori_loop(group + 1, groups, start_fetch, 0)

    key_cols = (slice(0, 128), slice(128, 384))
    value_cols = (slice(0, 256), slice(256, 384))
    value_width = (256, 128)
    parts = [
        (head, slice(first, first + chunk), first)
        for head in range(2)
        for first in range(0, rows, chunk)
    ]
    lanes = lane_ids((chunk, 128))

    def one_plane(h, q_ref, waits):
        plane = group * PAIR + h
        is_long = plane < long_planes
        low = jnp.where(is_long, 0, group - 1)
        masked_low = jnp.where(is_long, group, group - 1)
        count = group + 1 - low

        for first in range(0, rows, chunk):
            here = slice(first, first + chunk)
            q1 = q_ref[here, 128 : 128 + HD].astype(jnp.float32)
            q1 = jnp.concatenate([q1, jnp.zeros((chunk, 128 - HD), jnp.float32)], axis=1)
            q1 = pltpu.roll(q1, 64, 1)
            span = slice(first, first + chunk)
            qs[span, :128] = q_ref[here, :128]
            qs[span, 128:256] = jnp.where(lanes < 64, 0.0, q1).astype(jnp.bfloat16)
            qs[span, 256:] = jnp.where(lanes < 32, q1, 0.0).astype(jnp.bfloat16)

        peaks[...] = jnp.full_like(peaks, neg_large)
        totals[...] = jnp.zeros_like(totals)
        contexts[...] = jnp.zeros_like(contexts)

        if waits:
            lax.fori_loop(least, group + 1, wait_fetch, 0)

        def score(k, masked):
            for head, span, first in parts:
                s = lax.dot_general(
                    qs[span, key_cols[head]],
                    kv_ref[k, :KEYS, key_cols[head]],
                    (((1,), (1,)), ((), ())),
                    preferred_element_type=jnp.float32,
                )
                if masked:
                    shape = (chunk, KEYS)
                    row_ids = plane * rows + first + lax.broadcasted_iota(jnp.int32, shape, 0)
                    key_ids = (
                        (k * PAIR + member) * rows
                        + column * KEYS
                        + lax.broadcasted_iota(jnp.int32, shape, 1)
                    )
                    allowed = (key_ids <= row_ids) & (row_ids < ends_ref[pl.ds(k, 1), :])
                    s = jnp.where(allowed, s, neg_large)
                scores[k - low, head, span, :] = s
                peaks[head, span, :] = jnp.maximum(
                    peaks[head, span, :], jnp.maximum(s[:, :128], s[:, 128:])
                )

        def free_step(k, carry):
            score(k, False)
            return carry

        def masked_step(k, carry):
            score(k, True)
            return carry

        lax.fori_loop(low, masked_low, free_step, 0)
        lax.fori_loop(masked_low, group + 1, masked_step, 0)

        @pl.when(count % 2 == 1)
        def _():
            scores[count] = jnp.full(scores.shape[1:], neg_large, jnp.float32)

        tops = []
        for head, span, first in parts:
            top = jnp.max(peaks[head, span, :], axis=1, keepdims=True)
            tops.append(top)
            peaks[head, span, :] = jnp.broadcast_to(top * log2_scale, (chunk, 128))

        def weigh(i, carry):
            for head, span, first in parts:
                shift = peaks[head, span, :]
                total = totals[head, span, :]
                context = contexts[head, span, : value_width[head]]
                for n in range(2):
                    slot = 2 * i + n
                    k = jnp.minimum(low + slot, group)
                    s = scores[slot, head, span, :]
                    left = jnp.exp2(s[:, :128] * log2_scale - shift)
                    right = jnp.exp2(s[:, 128:] * log2_scale - shift)
                    total = total + (left + right)
                    p = jnp.concatenate(
                        [left.astype(jnp.bfloat16), right.astype(jnp.bfloat16)], axis=1
                    )
                    context = context + jnp.dot(
                        p, kv_ref[k, :KEYS, value_cols[head]], preferred_element_type=jnp.float32
                    )
                totals[head, span, :] = total
                contexts[head, span, : value_width[head]] = context
            return carry

        lax.fori_loop(0, (count + 1) // 2, weigh, 0)

        for first in range(0, rows, chunk):
            span = slice(first, first + chunk)
            found = []
            columns = []
            for head in range(2):
                top = tops[head * (rows // chunk) + first // chunk]
                denominator = jnp.sum(totals[head, span, :], axis=1, keepdims=True)
                if head == 0:
                    left = pltpu.roll(contexts[head, span, :128], 32, 1)
                    right = pltpu.roll(contexts[head, span, 128:], 32, 1)
                    context = jnp.where(lanes < 32, left, right)
                else:
                    context = pltpu.roll(contexts[head, span, :128], 96, 1)
                found.append(jnp.where(lanes < HD, context / denominator, 0.0))
                lse = top * score_scale + jnp.log(denominator)
                coarse = lse.astype(jnp.bfloat16).astype(jnp.float32)
                middle = (lse - coarse).astype(jnp.bfloat16).astype(jnp.float32)
                columns += [coarse, middle, lse - coarse - middle]
            target = h * MESH_Y + first // KEYS
            mid = chunk // 2
            packed = pack_heads(found[0][:mid], found[1][:mid], found[0][mid:], found[1][mid:])
            for i in range(3):
                out_ref[target, page_rows : page_rows + mid, 128 * i : 128 * i + 128] = packed[
                    i
                ].astype(jnp.bfloat16)
            spread = jnp.zeros((chunk, 128), jnp.float32)
            for i, value in enumerate(columns):
                spread = jnp.where(lanes == i, value, spread)
            tail = slice(page_rows + mid, page_rows + mid + 16)
            out_ref[target, tail, :chunk] = jnp.transpose(spread, (1, 0))[:16].astype(jnp.bfloat16)
            out_ref[target, tail, chunk:] = jnp.zeros((16, 384 - chunk), jnp.bfloat16)

    one_plane(member, own_ref, True)
    one_plane(1 - member, other_ref, False)

    lax.fori_loop(0, least, wait_fetch, 0)
    lax.fori_loop(group + 1, groups, wait_fetch, 0)
    shape = (targets * 16, KEYS)
    row = lax.broadcasted_iota(jnp.int32, shape, 0)
    key = lax.broadcasted_iota(jnp.int32, shape, 1)
    same_place = (row & 7) == (key & 7)
    parity = (row >> 3) & 1
    owner = (group * targets + (row >> 4)).astype(jnp.float32)
    for two in range(groups // 2):
        total = None
        for n in range(2):
            k = 2 * two + n
            owners = kv_ref[k, KEYS : KEYS + 16, :KEYS].astype(jnp.float32)[:1]
            chosen = (owners == owner) & same_place & (parity == n)
            picked = jnp.dot(
                jnp.where(chosen, 1.0, 0.0).astype(jnp.bfloat16),
                kv_ref[k, :KEYS, :],
                preferred_element_type=jnp.float32,
            )
            total = picked if total is None else total + picked
        total = total.astype(jnp.bfloat16)
        for t in range(targets):
            out_ref[t, 16 * two : 16 * two + 16, :] = total[16 * t : 16 * t + 16]


def combine(flag_ref, pages_ref, got_ref, att_ref, lse_ref, cache_ref):
    count = got_ref.shape[0]
    groups = cache_ref.shape[0]
    base = groups * CAP
    for t in range(count):
        cache_ref[:, t] = pages_ref[t, :groups]
    live = flag_ref[0] == 0
    mid = KEYS // 2
    shares = []
    for head in range(2):
        lses = []
        for i in range(count):
            rows = got_ref[i, base + mid : base + mid + 16, :KEYS].astype(jnp.float32)
            first = 3 * head
            lses.append(
                rows[first : first + 1] + rows[first + 1 : first + 2] + rows[first + 2 : first + 3]
            )
        lses = jnp.concatenate(lses, axis=0)
        peak = jnp.max(lses, axis=0, keepdims=True)
        weights = jnp.exp(lses - peak)
        total = jnp.sum(weights, axis=0, keepdims=True)
        shares.append(weights / total)
        lse_ref[head : head + 1, :] = jnp.where(live, peak + jnp.log(total), 0.0)
    shares.append(jnp.zeros((128 - 2 * count, KEYS), jnp.float32))
    shares = jnp.transpose(jnp.concatenate(shares, axis=0), (1, 0))
    lanes = lane_ids((mid, 128))
    sums = [None] * 3
    for i in range(count):
        near0, near1 = shares[:mid, i : i + 1], shares[:mid, count + i : count + i + 1]
        far0, far1 = shares[mid:, i : i + 1], shares[mid:, count + i : count + i + 1]
        spread = (
            jnp.where(lanes < 96, near0, near1),
            jnp.where(lanes < 64, near1, far0),
            jnp.where(lanes < 32, far0, far1),
        )
        for j in range(3):
            part = got_ref[i, base : base + mid, 128 * j : 128 * j + 128]
            part = part.astype(jnp.float32) * spread[j]
            sums[j] = part if sums[j] is None else sums[j] + part
    turned = [
        jnp.where(live, jnp.transpose(v, (1, 0)), 0.0).astype(jnp.bfloat16) for v in sums
    ]
    att_ref[:128, :mid] = turned[0]
    att_ref[128:, :mid] = turned[1][:64]
    att_ref[:64, mid:] = turned[1][64:]
    att_ref[64:, mid:] = turned[2]


SMEM = pl.BlockSpec(memory_space=pltpu.SMEM)
VMEM = pl.BlockSpec(memory_space=pltpu.VMEM)
ANY = pl.BlockSpec(memory_space=pl.ANY)
SMALL = pltpu.CompilerParams(vmem_limit_bytes=40 << 20)


def in_vmem(x):
    return pltpu.with_memory_space_constraint(x, pltpu.VMEM)


def in_hbm(x):
    return pltpu.with_memory_space_constraint(x, pltpu.HBM)


def body(stream_x, qkv_weight, short_lengths, cache_owner):
    groups, columns = lax.axis_size("q"), lax.axis_size("y")
    targets = PAIR * columns
    tok_count = stream_x.shape[0]
    group, member, column = lax.axis_index("q"), lax.axis_index("p"), lax.axis_index("y")
    plane = group * PAIR + member
    core = lax.axis_index("c").astype(jnp.int32).reshape(1)
    plane_rows = tok_count * columns
    long_planes = groups * PAIR * 11 // 16
    bounds = boundaries(short_lengths, plane_rows * long_planes)

    weight = in_vmem(qkv_weight.T)
    ours = lax.all_gather(stream_x, "x", axis=0, tiled=True)
    theirs = lax.ppermute(ours, "c", [(0, 1), (1, 0)])

    row_ids = (
        plane * plane_rows + column * tok_count + jnp.arange(tok_count, dtype=jnp.int32)
    )
    passed = row_ids[:, None] >= bounds[None, :]
    seg_begin = jnp.max(jnp.where(passed, bounds[None, :], 0), axis=1)
    position = (row_ids - seg_begin).astype(jnp.float32)
    half_dim = HD // 2
    lane = jnp.arange(128, dtype=jnp.int32)
    entry = jnp.where(lane < half_dim, lane, lane - half_dim)
    inverse_freq = rope_base ** (-entry.astype(jnp.float32) / half_dim)
    sign = jnp.where(lane < half_dim, -1.0, jnp.where(lane < HD, 1.0, 0.0))
    angle = position[:, None] * inverse_freq[None, :]
    cosine = jnp.where(lane[None, :] < HD, jnp.cos(angle), 0.0)
    sine = jnp.sin(angle) * sign[None, :]

    owner_row = jnp.where(row_ids < bounds[-1], cache_owner.reshape(tok_count), -1)
    owner_row = owner_row.astype(jnp.float32)[None, :]

    half = pl.pallas_call(
        half_projection,
        in_specs=[SMEM, VMEM, VMEM],
        out_specs=VMEM,
        out_shape=jax.ShapeDtypeStruct((tok_count, qkv_weight.shape[1]), jnp.float32),
        compiler_params=SMALL,
    )(core, in_vmem(ours), weight)
    early = 176
    queries, keys_early, keys_late = pl.pallas_call(
        rest_projection,
        in_specs=[SMEM] + [VMEM] * 6,
        out_specs=[VMEM, VMEM, VMEM],
        out_shape=[
            jax.ShapeDtypeStruct((tok_count, 128 + HD), jnp.bfloat16),
            jax.ShapeDtypeStruct((early, 384), jnp.bfloat16),
            jax.ShapeDtypeStruct((tok_count + 16 - early, 384), jnp.bfloat16),
        ],
        compiler_params=SMALL,
    )(1 - core, in_vmem(theirs), weight, in_vmem(half), in_vmem(cosine), in_vmem(sine), owner_row)

    gathered = lax.all_gather(keys_early, "q", axis=0, tiled=True)
    own_queries = lax.all_gather(queries, "y", axis=0, tiled=True)
    other_queries = lax.ppermute(own_queries, "p", [(0, 1), (1, 0)])
    own_queries, keys_late, short_lengths = lax.optimization_barrier(
        (own_queries, keys_late, short_lengths)
    )
    gathered_late = lax.all_gather(keys_late, "q", axis=0, tiled=True)

    bounds = boundaries(short_lengths, plane_rows * long_planes)
    key_ids = (
        (jnp.arange(groups, dtype=jnp.int32) * PAIR + member) * plane_rows + column * tok_count
    )[:, None] + jnp.arange(tok_count, dtype=jnp.int32)[None, :]
    ends = jnp.min(
        jnp.where(bounds[None, None, :] > key_ids[:, :, None], bounds[None, None, :], 1 << 30),
        axis=2,
    )

    info = jnp.stack([group, member, column]).astype(jnp.int32)
    padding = (row_ids[:1] >= bounds[-1]).astype(jnp.int32)
    gathered, gathered_late, own_queries, ends, info, padding = lax.optimization_barrier(
        (gathered, gathered_late, own_queries, ends, info, padding)
    )

    most = max((long_planes - 1) // PAIR + 1, 2)
    slots = 2 * ((most + 1) // 2)
    page_rows = groups * CAP
    box_rows = page_rows + tok_count // 2 + 16
    outbox = pl.pallas_call(
        attention,
        in_specs=[SMEM, VMEM, VMEM, VMEM, ANY, ANY],
        out_specs=VMEM,
        out_shape=jax.ShapeDtypeStruct((targets, box_rows, 384), jnp.bfloat16),
        scratch_shapes=[
            pltpu.VMEM((groups, tok_count + 16, 384), jnp.bfloat16),
            pltpu.VMEM((plane_rows, 384), jnp.bfloat16),
            pltpu.VMEM((slots, 2, plane_rows, 256), jnp.float32),
            pltpu.VMEM((2, plane_rows, 128), jnp.float32),
            pltpu.VMEM((2, plane_rows, 128), jnp.float32),
            pltpu.VMEM((2, plane_rows, 256), jnp.float32),
            pltpu.SemaphoreType.DMA((groups, 2)),
        ],
    )(
        info,
        own_queries,
        other_queries,
        ends,
        gathered.reshape(groups, early, 384),
        gathered_late.reshape(groups, tok_count + 16 - early, 384),
    )
    received = lax.all_to_all(outbox, ("p", "y"), split_axis=0, concat_axis=0, tiled=True)
    attended, row_lse, kv_cache = pl.pallas_call(
        combine,
        in_specs=[SMEM, VMEM, VMEM],
        out_specs=[VMEM, VMEM, VMEM],
        out_shape=[
            jax.ShapeDtypeStruct((2 * HD, tok_count), jnp.bfloat16),
            jax.ShapeDtypeStruct((2, tok_count), jnp.float32),
            jax.ShapeDtypeStruct((groups, targets, CAP, 384), jnp.bfloat16),
        ],
        compiler_params=SMALL,
    )(
        padding,
        in_vmem(received.reshape(targets, box_rows // CAP, CAP, 384)),
        in_vmem(received),
    )
    return (attended.T, row_lse, kv_cache.reshape(-1, 384))


def solution(mesh):
    seq, head = mesh.devices.shape
    shape = (seq // (MESH_Y * PAIR), PAIR, MESH_Y, head // 2, 2)
    fine = Mesh(mesh.devices.reshape(shape), ("q", "p", "y", "x", "c"))
    seq_axes, head_axes = ("q", "p", "y"), ("x", "c")
    return jax.shard_map(
        body,
        mesh=fine,
        in_specs=(P(seq_axes, head_axes), P(None, head_axes), P(), P(seq_axes, None)),
        out_specs=(P(seq_axes, head_axes), P(head_axes, seq_axes), P(seq_axes, head_axes)),
        check_vma=False,
    )
```

```python
import functools
import math

import jax
import jax.numpy as jnp
from jax import lax
from jax.experimental import pallas as pl
from jax.experimental.pallas import tpu as pltpu
from jax.sharding import Mesh, PartitionSpec as P

HD = 96
CAP = 8
neg_large = -1e30
rope_base = 10000.0
score_scale = 1.0 / math.sqrt(HD)
log2_scale = score_scale * math.log2(math.e)


def boundaries(short_lengths, long_length):
    count = short_lengths.shape[0]
    before = jnp.arange(count)[None, :] < jnp.arange(count + 1)[:, None]
    return jnp.sum(jnp.where(before, short_lengths[None, :], 0), axis=1) + long_length


PAIR = 2
KEYS = 256
MESH_Y = 4


def lane_ids(shape):
    return lax.broadcasted_iota(jnp.int32, shape, 1)


def block_sum(core, x_ref, w_ref):
    rows = 256
    depth = x_ref.shape[1]
    total = None
    for i in range(x_ref.shape[0] // rows):
        first = pl.multiple_of((2 * i + core) * depth, 128)
        part = lax.dot_general(
            x_ref[i * rows : (i + 1) * rows, :],
            w_ref[:, pl.ds(first, depth)],
            (((1,), (1,)), ((), ())),
            preferred_element_type=jnp.float32,
        )
        total = part if total is None else total + part
    return total


def half_projection(core_ref, x_ref, w_ref, out_ref):
    out_ref[...] = block_sum(core_ref[0], x_ref, w_ref)


def pack_heads(p0, p1, p2, p3):
    lanes = lane_ids(p0.shape)
    r1 = pltpu.roll(p1, 96, 1)
    r2 = pltpu.roll(p2, 64, 1)
    r3 = pltpu.roll(p3, 32, 1)
    return (
        jnp.where(lanes < 96, p0, r1),
        jnp.where(lanes < 64, r1, r2),
        jnp.where(lanes < 32, r2, r3),
    )


def rest_projection(
    core_ref, x_ref, w_ref, first_ref, cos_ref, sin_ref, owner_ref, q_ref, kv_ref
):
    total = first_ref[...] + block_sum(core_ref[0], x_ref, w_ref)
    rows, columns = total.shape
    width = columns + 64
    whole = jnp.concatenate([total, jnp.zeros((rows, 64), jnp.float32)], axis=1)
    cosine = cos_ref[...]
    sine = sin_ref[...]
    lanes = lane_ids((rows, 128))

    def window(first):
        return pltpu.roll(whole, (width - first) % width, 1)[:, :128]

    def rotated(first):
        here = window(first)
        ahead = window(first + 48)
        behind = window((first - 48) % width)
        return here * cosine + jnp.where(lanes < 48, ahead, behind) * sine

    def plain(first):
        return jnp.where(lanes < HD, window(first), 0.0)

    key_values = pack_heads(rotated(96), plain(192), rotated(384), plain(480))
    for i in range(3):
        kv_ref[:rows, 128 * i : 128 * i + 128] = key_values[i].astype(jnp.bfloat16)
    kv_ref[rows:, :rows] = jnp.broadcast_to(owner_ref[...], (16, rows)).astype(jnp.bfloat16)
    kv_ref[rows:, rows:] = jnp.zeros((16, 384 - rows), jnp.bfloat16)
    q_ref[:, :128] = rotated(0).astype(jnp.bfloat16)
    q_ref[:, 128:] = rotated(288)[:, :HD].astype(jnp.bfloat16)


def attention(
    info_ref,
    own_ref,
    other_ref,
    ends_ref,
    kv_hbm,
    out_ref,
    kv_ref,
    qs,
    scores,
    peaks,
    totals,
    contexts,
    kv_sems,
):
    group, member, column = info_ref[0], info_ref[1], info_ref[2]
    groups = kv_ref.shape[0]
    rows = MESH_Y * KEYS
    chunk = 256
    targets = out_ref.shape[0]
    page_rows = groups * CAP
    long_planes = 11 * groups * PAIR // 16

    def fetch(k):
        return pltpu.make_async_copy(kv_hbm.at[k], kv_ref.at[k], kv_sems.at[k])

    least = jnp.where(group * PAIR < long_planes, 0, group - 1)

    def start_fetch(k, carry):
        fetch(k).start()
        return carry

    def wait_fetch(k, carry):
        fetch(k).wait()
        return carry

    lax.fori_loop(least, group + 1, start_fetch, 0)
    lax.fori_loop(0, least, start_fetch, 0)
    lax.fori_loop(group + 1, groups, start_fetch, 0)

    key_cols = (slice(0, 128), slice(128, 384))
    value_cols = (slice(0, 256), slice(256, 384))
    value_width = (256, 128)
    parts = [
        (head, slice(first, first + chunk), first)
        for head in range(2)
        for first in range(0, rows, chunk)
    ]
    lanes = lane_ids((chunk, 128))

    def one_plane(h, q_ref, waits):
        plane = group * PAIR + h
        is_long = plane < long_planes
        low = jnp.where(is_long, 0, group - 1)
        masked_low = jnp.where(is_long, group, group - 1)
        count = group + 1 - low

        for first in range(0, rows, chunk):
            here = slice(first, first + chunk)
            q1 = q_ref[here, 128 : 128 + HD].astype(jnp.float32)
            q1 = jnp.concatenate([q1, jnp.zeros((chunk, 128 - HD), jnp.float32)], axis=1)
            q1 = pltpu.roll(q1, 64, 1)
            span = slice(first, first + chunk)
            qs[span, :128] = q_ref[here, :128]
            qs[span, 128:256] = jnp.where(lanes < 64, 0.0, q1).astype(jnp.bfloat16)
            qs[span, 256:] = jnp.where(lanes < 32, q1, 0.0).astype(jnp.bfloat16)

        peaks[...] = jnp.full_like(peaks, neg_large)
        totals[...] = jnp.zeros_like(totals)
        contexts[...] = jnp.zeros_like(contexts)

        if waits:
            lax.fori_loop(least, group + 1, wait_fetch, 0)

        def score(k, masked):
            for head, span, first in parts:
                s = lax.dot_general(
                    qs[span, key_cols[head]],
                    kv_ref[k, :KEYS, key_cols[head]],
                    (((1,), (1,)), ((), ())),
                    preferred_element_type=jnp.float32,
                )
                if masked:
                    shape = (chunk, KEYS)
                    row_ids = plane * rows + first + lax.broadcasted_iota(jnp.int32, shape, 0)
                    key_ids = (
                        (k * PAIR + member) * rows
                        + column * KEYS
                        + lax.broadcasted_iota(jnp.int32, shape, 1)
                    )
                    allowed = (key_ids <= row_ids) & (row_ids < ends_ref[pl.ds(k, 1), :])
                    s = jnp.where(allowed, s, neg_large)
                scores[k - low, head, span, :] = s
                peaks[head, span, :] = jnp.maximum(
                    peaks[head, span, :], jnp.maximum(s[:, :128], s[:, 128:])
                )

        def free_step(k, carry):
            score(k, False)
            return carry

        def masked_step(k, carry):
            score(k, True)
            return carry

        lax.fori_loop(low, masked_low, free_step, 0)
        lax.fori_loop(masked_low, group + 1, masked_step, 0)

        @pl.when(count % 2 == 1)
        def _():
            scores[count] = jnp.full(scores.shape[1:], neg_large, jnp.float32)

        tops = []
        for head, span, first in parts:
            top = jnp.max(peaks[head, span, :], axis=1, keepdims=True)
            tops.append(top)
            peaks[head, span, :] = jnp.broadcast_to(top * log2_scale, (chunk, 128))

        def weigh(i, carry):
            for head, span, first in parts:
                shift = peaks[head, span, :]
                total = totals[head, span, :]
                context = contexts[head, span, : value_width[head]]
                for n in range(2):
                    slot = 2 * i + n
                    k = jnp.minimum(low + slot, group)
                    s = scores[slot, head, span, :]
                    left = jnp.exp2(s[:, :128] * log2_scale - shift)
                    right = jnp.exp2(s[:, 128:] * log2_scale - shift)
                    total = total + (left + right)
                    p = jnp.concatenate(
                        [left.astype(jnp.bfloat16), right.astype(jnp.bfloat16)], axis=1
                    )
                    context = context + jnp.dot(
                        p, kv_ref[k, :KEYS, value_cols[head]], preferred_element_type=jnp.float32
                    )
                totals[head, span, :] = total
                contexts[head, span, : value_width[head]] = context
            return carry

        lax.fori_loop(0, (count + 1) // 2, weigh, 0)

        for first in range(0, rows, chunk):
            span = slice(first, first + chunk)
            found = []
            columns = []
            for head in range(2):
                top = tops[head * (rows // chunk) + first // chunk]
                denominator = jnp.sum(totals[head, span, :], axis=1, keepdims=True)
                if head == 0:
                    left = pltpu.roll(contexts[head, span, :128], 32, 1)
                    right = pltpu.roll(contexts[head, span, 128:], 32, 1)
                    context = jnp.where(lanes < 32, left, right)
                else:
                    context = pltpu.roll(contexts[head, span, :128], 96, 1)
                found.append(jnp.where(lanes < HD, context / denominator, 0.0))
                lse = top * score_scale + jnp.log(denominator)
                coarse = lse.astype(jnp.bfloat16).astype(jnp.float32)
                middle = (lse - coarse).astype(jnp.bfloat16).astype(jnp.float32)
                columns += [coarse, middle, lse - coarse - middle]
            target = h * MESH_Y + first // KEYS
            mid = chunk // 2
            packed = pack_heads(found[0][:mid], found[1][:mid], found[0][mid:], found[1][mid:])
            for i in range(3):
                out_ref[target, page_rows : page_rows + mid, 128 * i : 128 * i + 128] = packed[
                    i
                ].astype(jnp.bfloat16)
            spread = jnp.zeros((chunk, 128), jnp.float32)
            for i, value in enumerate(columns):
                spread = jnp.where(lanes == i, value, spread)
            tail = slice(page_rows + mid, page_rows + mid + 16)
            out_ref[target, tail, :chunk] = jnp.transpose(spread, (1, 0))[:16].astype(jnp.bfloat16)
            out_ref[target, tail, chunk:] = jnp.zeros((16, 384 - chunk), jnp.bfloat16)

    one_plane(member, own_ref, True)
    one_plane(1 - member, other_ref, False)

    lax.fori_loop(0, least, wait_fetch, 0)
    lax.fori_loop(group + 1, groups, wait_fetch, 0)
    shape = (targets * 16, KEYS)
    row = lax.broadcasted_iota(jnp.int32, shape, 0)
    key = lax.broadcasted_iota(jnp.int32, shape, 1)
    same_place = (row & 7) == (key & 7)
    parity = (row >> 3) & 1
    owner = (group * targets + (row >> 4)).astype(jnp.float32)
    for two in range(groups // 2):
        total = None
        for n in range(2):
            k = 2 * two + n
            owners = kv_ref[k, KEYS : KEYS + 16, :KEYS].astype(jnp.float32)[:1]
            chosen = (owners == owner) & same_place & (parity == n)
            picked = jnp.dot(
                jnp.where(chosen, 1.0, 0.0).astype(jnp.bfloat16),
                kv_ref[k, :KEYS, :],
                preferred_element_type=jnp.float32,
            )
            total = picked if total is None else total + picked
        total = total.astype(jnp.bfloat16)
        for t in range(targets):
            out_ref[t, 16 * two : 16 * two + 16, :] = total[16 * t : 16 * t + 16]


def combine(flag_ref, pages_ref, got_ref, att_ref, lse_ref, cache_ref):
    count = got_ref.shape[0]
    groups = cache_ref.shape[0]
    base = groups * CAP
    for t in range(count):
        cache_ref[:, t] = pages_ref[t, :groups]
    live = flag_ref[0] == 0
    mid = KEYS // 2
    shares = []
    for head in range(2):
        lses = []
        for i in range(count):
            rows = got_ref[i, base + mid : base + mid + 16, :KEYS].astype(jnp.float32)
            first = 3 * head
            lses.append(
                rows[first : first + 1] + rows[first + 1 : first + 2] + rows[first + 2 : first + 3]
            )
        lses = jnp.concatenate(lses, axis=0)
        peak = jnp.max(lses, axis=0, keepdims=True)
        weights = jnp.exp(lses - peak)
        total = jnp.sum(weights, axis=0, keepdims=True)
        shares.append(weights / total)
        lse_ref[head : head + 1, :] = jnp.where(live, peak + jnp.log(total), 0.0)
    shares.append(jnp.zeros((128 - 2 * count, KEYS), jnp.float32))
    shares = jnp.transpose(jnp.concatenate(shares, axis=0), (1, 0))
    lanes = lane_ids((mid, 128))
    sums = [None] * 3
    for i in range(count):
        near0, near1 = shares[:mid, i : i + 1], shares[:mid, count + i : count + i + 1]
        far0, far1 = shares[mid:, i : i + 1], shares[mid:, count + i : count + i + 1]
        spread = (
            jnp.where(lanes < 96, near0, near1),
            jnp.where(lanes < 64, near1, far0),
            jnp.where(lanes < 32, far0, far1),
        )
        for j in range(3):
            part = got_ref[i, base : base + mid, 128 * j : 128 * j + 128]
            part = part.astype(jnp.float32) * spread[j]
            sums[j] = part if sums[j] is None else sums[j] + part
    turned = [
        jnp.where(live, jnp.transpose(v, (1, 0)), 0.0).astype(jnp.bfloat16) for v in sums
    ]
    att_ref[:128, :mid] = turned[0]
    att_ref[128:, :mid] = turned[1][:64]
    att_ref[:64, mid:] = turned[1][64:]
    att_ref[64:, mid:] = turned[2]


SMEM = pl.BlockSpec(memory_space=pltpu.SMEM)
VMEM = pl.BlockSpec(memory_space=pltpu.VMEM)
ANY = pl.BlockSpec(memory_space=pl.ANY)
SMALL = pltpu.CompilerParams(vmem_limit_bytes=40 << 20)


def in_vmem(x):
    return pltpu.with_memory_space_constraint(x, pltpu.VMEM)


def in_hbm(x):
    return pltpu.with_memory_space_constraint(x, pltpu.HBM)


def body(stream_x, qkv_weight, short_lengths, cache_owner):
    groups, columns = lax.axis_size("q"), lax.axis_size("y")
    targets = PAIR * columns
    tok_count = stream_x.shape[0]
    group, member, column = lax.axis_index("q"), lax.axis_index("p"), lax.axis_index("y")
    plane = group * PAIR + member
    core = lax.axis_index("c").astype(jnp.int32).reshape(1)
    plane_rows = tok_count * columns
    long_planes = groups * PAIR * 11 // 16
    bounds = boundaries(short_lengths, plane_rows * long_planes)

    weight = in_vmem(qkv_weight.T)
    ours = lax.all_gather(stream_x, "x", axis=0, tiled=True)
    theirs = lax.ppermute(ours, "c", [(0, 1), (1, 0)])

    row_ids = (
        plane * plane_rows + column * tok_count + jnp.arange(tok_count, dtype=jnp.int32)
    )
    passed = row_ids[:, None] >= bounds[None, :]
    seg_begin = jnp.max(jnp.where(passed, bounds[None, :], 0), axis=1)
    position = (row_ids - seg_begin).astype(jnp.float32)
    half_dim = HD // 2
    lane = jnp.arange(128, dtype=jnp.int32)
    entry = jnp.where(lane < half_dim, lane, lane - half_dim)
    inverse_freq = rope_base ** (-entry.astype(jnp.float32) / half_dim)
    sign = jnp.where(lane < half_dim, -1.0, jnp.where(lane < HD, 1.0, 0.0))
    angle = position[:, None] * inverse_freq[None, :]
    cosine = jnp.where(lane[None, :] < HD, jnp.cos(angle), 0.0)
    sine = jnp.sin(angle) * sign[None, :]

    owner_row = jnp.where(row_ids < bounds[-1], cache_owner.reshape(tok_count), -1)
    owner_row = owner_row.astype(jnp.float32)[None, :]

    half = pl.pallas_call(
        half_projection,
        in_specs=[SMEM, VMEM, VMEM],
        out_specs=VMEM,
        out_shape=jax.ShapeDtypeStruct((tok_count, qkv_weight.shape[1]), jnp.float32),
        compiler_params=SMALL,
    )(core, in_vmem(ours), weight)
    queries, key_values = pl.pallas_call(
        rest_projection,
        in_specs=[SMEM] + [VMEM] * 6,
        out_specs=[VMEM, VMEM],
        out_shape=[
            jax.ShapeDtypeStruct((tok_count, 128 + HD), jnp.bfloat16),
            jax.ShapeDtypeStruct((tok_count + 16, 384), jnp.bfloat16),
        ],
        compiler_params=SMALL,
    )(1 - core, in_vmem(theirs), weight, in_vmem(half), in_vmem(cosine), in_vmem(sine), owner_row)

    gathered = lax.all_gather(key_values, "q", axis=0, tiled=True)
    own_queries = lax.all_gather(queries, "y", axis=0, tiled=True)
    other_queries = lax.ppermute(own_queries, "p", [(0, 1), (1, 0)])
    own_queries, short_lengths = lax.optimization_barrier((own_queries, short_lengths))

    bounds = boundaries(short_lengths, plane_rows * long_planes)
    key_ids = (
        (jnp.arange(groups, dtype=jnp.int32) * PAIR + member) * plane_rows + column * tok_count
    )[:, None] + jnp.arange(tok_count, dtype=jnp.int32)[None, :]
    ends = jnp.min(
        jnp.where(bounds[None, None, :] > key_ids[:, :, None], bounds[None, None, :], 1 << 30),
        axis=2,
    )

    info = jnp.stack([group, member, column]).astype(jnp.int32)
    padding = (row_ids[:1] >= bounds[-1]).astype(jnp.int32)
    gathered, own_queries, other_queries, ends, info, padding = lax.optimization_barrier(
        (gathered, own_queries, other_queries, ends, info, padding)
    )

    most = max((long_planes - 1) // PAIR + 1, 2)
    slots = 2 * ((most + 1) // 2)
    page_rows = groups * CAP
    box_rows = page_rows + tok_count // 2 + 16
    outbox = pl.pallas_call(
        attention,
        in_specs=[SMEM, VMEM, VMEM, VMEM, ANY],
        out_specs=VMEM,
        out_shape=jax.ShapeDtypeStruct((targets, box_rows, 384), jnp.bfloat16),
        scratch_shapes=[
            pltpu.VMEM((groups, tok_count + 16, 384), jnp.bfloat16),
            pltpu.VMEM((plane_rows, 384), jnp.bfloat16),
            pltpu.VMEM((slots, 2, plane_rows, 256), jnp.float32),
            pltpu.VMEM((2, plane_rows, 128), jnp.float32),
            pltpu.VMEM((2, plane_rows, 128), jnp.float32),
            pltpu.VMEM((2, plane_rows, 256), jnp.float32),
            pltpu.SemaphoreType.DMA((groups,)),
        ],
    )(
        info,
        own_queries,
        other_queries,
        ends,
        gathered.reshape(groups, tok_count + 16, 384),
    )
    received = lax.all_to_all(outbox, ("p", "y"), split_axis=0, concat_axis=0, tiled=True)
    attended, row_lse, kv_cache = pl.pallas_call(
        combine,
        in_specs=[SMEM, VMEM, VMEM],
        out_specs=[VMEM, VMEM, VMEM],
        out_shape=[
            jax.ShapeDtypeStruct((2 * HD, tok_count), jnp.bfloat16),
            jax.ShapeDtypeStruct((2, tok_count), jnp.float32),
            jax.ShapeDtypeStruct((groups, targets, CAP, 384), jnp.bfloat16),
        ],
        compiler_params=SMALL,
    )(
        padding,
        in_vmem(received.reshape(targets, box_rows // CAP, CAP, 384)),
        in_vmem(received),
    )
    return (attended.T, row_lse, kv_cache.reshape(-1, 384))


def solution(mesh):
    seq, head = mesh.devices.shape
    shape = (seq // (MESH_Y * PAIR), PAIR, MESH_Y, head // 2, 2)
    fine = Mesh(mesh.devices.reshape(shape), ("q", "p", "y", "x", "c"))
    seq_axes, head_axes = ("q", "p", "y"), ("x", "c")
    return jax.shard_map(
        body,
        mesh=fine,
        in_specs=(P(seq_axes, head_axes), P(None, head_axes), P(), P(seq_axes, None)),
        out_specs=(P(seq_axes, head_axes), P(head_axes, seq_axes), P(seq_axes, head_axes)),
        check_vma=False,
    )
```

```python
import functools
import math

import jax
import jax.numpy as jnp
from jax import lax
from jax.experimental import pallas as pl
from jax.experimental.pallas import tpu as pltpu
from jax.sharding import Mesh, PartitionSpec as P

HD = 96
CAP = 8
neg_large = -1e30
rope_base = 10000.0
score_scale = 1.0 / math.sqrt(HD)
log2_scale = score_scale * math.log2(math.e)


def boundaries(short_lengths, long_length):
    count = short_lengths.shape[0]
    before = jnp.arange(count)[None, :] < jnp.arange(count + 1)[:, None]
    return jnp.sum(jnp.where(before, short_lengths[None, :], 0), axis=1) + long_length


PAIR = 2
KEYS = 256
SHORT_SUM = 4096
MESH_Y = 4


def lane_ids(shape):
    return lax.broadcasted_iota(jnp.int32, shape, 1)


def block_sum(core, x_ref, w_ref):
    rows = 256
    depth = x_ref.shape[1]
    total = None
    for i in range(x_ref.shape[0] // rows):
        first = pl.multiple_of((2 * i + core) * depth, 128)
        part = lax.dot_general(
            x_ref[i * rows : (i + 1) * rows, :],
            w_ref[:, pl.ds(first, depth)],
            (((1,), (1,)), ((), ())),
            preferred_element_type=jnp.float32,
        )
        total = part if total is None else total + part
    return total


def half_projection(core_ref, x_ref, w_ref, out_ref):
    out_ref[...] = block_sum(core_ref[0], x_ref, w_ref)


def pack_heads(p0, p1, p2, p3):
    lanes = lane_ids(p0.shape)
    r1 = pltpu.roll(p1, 96, 1)
    r2 = pltpu.roll(p2, 64, 1)
    r3 = pltpu.roll(p3, 32, 1)
    return (
        jnp.where(lanes < 96, p0, r1),
        jnp.where(lanes < 64, r1, r2),
        jnp.where(lanes < 32, r2, r3),
    )


def rest_projection(
    core_ref, x_ref, w_ref, first_ref, cos_ref, sin_ref, owner_ref, q_ref, kv_ref
):
    total = first_ref[...] + block_sum(core_ref[0], x_ref, w_ref)
    rows, columns = total.shape
    width = columns + 64
    whole = jnp.concatenate([total, jnp.zeros((rows, 64), jnp.float32)], axis=1)
    cosine = cos_ref[...]
    sine = sin_ref[...]
    lanes = lane_ids((rows, 128))

    def window(first):
        return pltpu.roll(whole, (width - first) % width, 1)[:, :128]

    def rotated(first):
        here = window(first)
        ahead = window(first + 48)
        behind = window((first - 48) % width)
        return here * cosine + jnp.where(lanes < 48, ahead, behind) * sine

    def plain(first):
        return jnp.where(lanes < HD, window(first), 0.0)

    key_values = pack_heads(rotated(96), plain(192), rotated(384), plain(480))
    for i in range(3):
        kv_ref[:rows, 128 * i : 128 * i + 128] = key_values[i].astype(jnp.bfloat16)
    kv_ref[rows:, :rows] = jnp.broadcast_to(owner_ref[...], (16, rows)).astype(jnp.bfloat16)
    kv_ref[rows:, rows:] = jnp.zeros((16, 384 - rows), jnp.bfloat16)
    q_ref[:, :128] = rotated(0).astype(jnp.bfloat16)
    q_ref[:, 128:] = rotated(288)[:, :HD].astype(jnp.bfloat16)


def attention(
    info_ref,
    own_ref,
    other_ref,
    ends_ref,
    kv_hbm,
    out_ref,
    kv_ref,
    qs,
    scores,
    peaks,
    totals,
    contexts,
    kv_sems,
):
    group, member, column = info_ref[0], info_ref[1], info_ref[2]
    groups = kv_ref.shape[0]
    rows = MESH_Y * KEYS
    chunk = 256
    targets = out_ref.shape[0]
    page_rows = groups * CAP
    long_planes = 11 * groups * PAIR // 16

    def fetch(k):
        return pltpu.make_async_copy(kv_hbm.at[k], kv_ref.at[k], kv_sems.at[k])

    least = jnp.where(group * PAIR < long_planes, 0, group - 1)

    def start_fetch(k, carry):
        fetch(k).start()
        return carry

    def wait_fetch(k, carry):
        fetch(k).wait()
        return carry

    lax.fori_loop(least, group + 1, start_fetch, 0)
    lax.fori_loop(0, least, start_fetch, 0)
    lax.fori_loop(group + 1, groups, start_fetch, 0)

    key_cols = (slice(0, 128), slice(128, 384))
    value_cols = (slice(0, 256), slice(256, 384))
    value_width = (256, 128)
    parts = [
        (head, slice(first, first + chunk), first)
        for head in range(2)
        for first in range(0, rows, chunk)
    ]
    lanes = lane_ids((chunk, 128))

    def one_plane(h, q_ref, waits):
        plane = group * PAIR + h
        is_long = plane < long_planes
        low = jnp.where(is_long, 0, group - 1)
        masked_low = jnp.where(is_long, group, group - 1)

        for first in range(0, rows, chunk):
            here = slice(first, first + chunk)
            q1 = q_ref[here, 128 : 128 + HD].astype(jnp.float32)
            q1 = jnp.concatenate([q1, jnp.zeros((chunk, 128 - HD), jnp.float32)], axis=1)
            q1 = pltpu.roll(q1, 64, 1)
            span = slice(first, first + chunk)
            qs[span, :128] = q_ref[here, :128]
            qs[span, 128:256] = jnp.where(lanes < 64, 0.0, q1).astype(jnp.bfloat16)
            qs[span, 256:] = jnp.where(lanes < 32, q1, 0.0).astype(jnp.bfloat16)

        if waits:
            lax.fori_loop(least, group + 1, wait_fetch, 0)

        def score(k, masked, fresh=False):
            for head, span, first in parts:
                s = lax.dot_general(
                    qs[span, key_cols[head]],
                    kv_ref[k, :KEYS, key_cols[head]],
                    (((1,), (1,)), ((), ())),
                    preferred_element_type=jnp.float32,
                )
                if masked:
                    shape = (chunk, KEYS)
                    row_ids = plane * rows + first + lax.broadcasted_iota(jnp.int32, shape, 0)
                    key_ids = (
                        (k * PAIR + member) * rows
                        + column * KEYS
                        + lax.broadcasted_iota(jnp.int32, shape, 1)
                    )
                    allowed = (key_ids <= row_ids) & (row_ids < ends_ref[pl.ds(k, 1), :])
                    s = jnp.where(allowed, s, neg_large)
                scores[k - low, head, span, :] = s
                top = jnp.maximum(s[:, :128], s[:, 128:])
                if not fresh:
                    top = jnp.maximum(peaks[head, span, :], top)
                peaks[head, span, :] = top

        def free_step(k, carry):
            score(k, False)
            return carry

        def masked_step(k, carry):
            score(k, True)
            return carry

        score(group, True, True)
        lax.fori_loop(low, masked_low, free_step, 0)
        lax.fori_loop(masked_low, group, masked_step, 0)

        tops = []
        for head, span, first in parts:
            top = jnp.max(peaks[head, span, :], axis=1, keepdims=True)
            tops.append(top)
            peaks[head, span, :] = jnp.broadcast_to(top * log2_scale, (chunk, 128))

        def weigh(k, fresh):
            for head, span, first in parts:
                shift = peaks[head, span, :]
                s = scores[k - low, head, span, :]
                left = jnp.exp2(s[:, :128] * log2_scale - shift)
                right = jnp.exp2(s[:, 128:] * log2_scale - shift)
                total = left + right
                p = jnp.concatenate([left.astype(jnp.bfloat16), right.astype(jnp.bfloat16)], axis=1)
                context = jnp.dot(
                    p, kv_ref[k, :KEYS, value_cols[head]], preferred_element_type=jnp.float32
                )
                if not fresh:
                    total = totals[head, span, :] + total
                    context = contexts[head, span, : value_width[head]] + context
                totals[head, span, :] = total
                contexts[head, span, : value_width[head]] = context

        def weigh_step(k, carry):
            weigh(k, False)
            return carry

        weigh(group, True)
        lax.fori_loop(low, group, weigh_step, 0)

        for first in range(0, rows, chunk):
            span = slice(first, first + chunk)
            found = []
            spread = jnp.zeros((chunk, 128), jnp.float32)
            for head in range(2):
                top = tops[head * (rows // chunk) + first // chunk]
                denominator = jnp.sum(totals[head, span, :], axis=1, keepdims=True)
                if head == 0:
                    left = pltpu.roll(contexts[head, span, :128], 32, 1)
                    right = pltpu.roll(contexts[head, span, 128:], 32, 1)
                    context = jnp.where(lanes < 32, left, right)
                else:
                    context = pltpu.roll(contexts[head, span, :128], 96, 1)
                found.append(jnp.where(lanes < HD, context / denominator, 0.0))
                spread = jnp.where(lanes == 2 * head, top, spread)
                spread = jnp.where(lanes == 2 * head + 1, denominator, spread)
            turned = jnp.transpose(spread, (1, 0))
            pieces = []
            for head in range(2):
                lse = turned[2 * head : 2 * head + 1] * score_scale + jnp.log(
                    turned[2 * head + 1 : 2 * head + 2]
                )
                coarse = lse.astype(jnp.bfloat16).astype(jnp.float32)
                middle = (lse - coarse).astype(jnp.bfloat16).astype(jnp.float32)
                pieces += [coarse, middle, lse - coarse - middle]
            pieces.append(jnp.zeros((10, chunk), jnp.float32))
            pieces = jnp.concatenate(pieces, axis=0).astype(jnp.bfloat16)
            target = h * MESH_Y + first // KEYS
            mid = chunk // 2
            packed = pack_heads(found[0][:mid], found[1][:mid], found[0][mid:], found[1][mid:])
            for i in range(3):
                out_ref[target, page_rows : page_rows + mid, 128 * i : 128 * i + 128] = packed[
                    i
                ].astype(jnp.bfloat16)
            tail = slice(page_rows + mid, page_rows + mid + 16)
            out_ref[target, tail, :chunk] = pieces
            out_ref[target, tail, chunk:] = jnp.zeros((16, 384 - chunk), jnp.bfloat16)

    one_plane(member, own_ref, True)
    one_plane(1 - member, other_ref, False)

    lax.fori_loop(0, least, wait_fetch, 0)
    lax.fori_loop(group + 1, groups, wait_fetch, 0)
    shape = (targets * 16, KEYS)
    row = lax.broadcasted_iota(jnp.int32, shape, 0)
    key = lax.broadcasted_iota(jnp.int32, shape, 1)
    same_place = (row & 7) == (key & 7)
    parity = (row >> 3) & 1
    owner = (group * targets + (row >> 4)).astype(jnp.float32)
    for two in range(groups // 2):
        total = None
        for n in range(2):
            k = 2 * two + n
            owners = kv_ref[k, KEYS : KEYS + 16, :KEYS].astype(jnp.float32)[:1]
            chosen = (owners == owner) & same_place & (parity == n)
            picked = jnp.dot(
                jnp.where(chosen, 1.0, 0.0).astype(jnp.bfloat16),
                kv_ref[k, :KEYS, :],
                preferred_element_type=jnp.float32,
            )
            total = picked if total is None else total + picked
        total = total.astype(jnp.bfloat16)
        for t in range(targets):
            out_ref[t, 16 * two : 16 * two + 16, :] = total[16 * t : 16 * t + 16]


def combine(flag_ref, pages_ref, got_ref, att_ref, lse_ref, cache_ref):
    count = got_ref.shape[0]
    groups = cache_ref.shape[0]
    base = groups * CAP
    for t in range(count):
        cache_ref[:, t] = pages_ref[t, :groups]
    live = flag_ref[0] == 0
    mid = KEYS // 2
    shares = []
    for head in range(2):
        lses = []
        for i in range(count):
            rows = got_ref[i, base + mid : base + mid + 16, :KEYS].astype(jnp.float32)
            first = 3 * head
            lses.append(
                rows[first : first + 1] + rows[first + 1 : first + 2] + rows[first + 2 : first + 3]
            )
        lses = jnp.concatenate(lses, axis=0)
        peak = jnp.max(lses, axis=0, keepdims=True)
        weights = jnp.exp(lses - peak)
        total = jnp.sum(weights, axis=0, keepdims=True)
        shares.append(weights / total)
        lse_ref[head : head + 1, :] = jnp.where(live, peak + jnp.log(total), 0.0)
    shares.append(jnp.zeros((128 - 2 * count, KEYS), jnp.float32))
    shares = jnp.transpose(jnp.concatenate(shares, axis=0), (1, 0))
    lanes = lane_ids((mid, 128))
    sums = [None] * 3
    for i in range(count):
        near0, near1 = shares[:mid, i : i + 1], shares[:mid, count + i : count + i + 1]
        far0, far1 = shares[mid:, i : i + 1], shares[mid:, count + i : count + i + 1]
        spread = (
            jnp.where(lanes < 96, near0, near1),
            jnp.where(lanes < 64, near1, far0),
            jnp.where(lanes < 32, far0, far1),
        )
        for j in range(3):
            part = got_ref[i, base : base + mid, 128 * j : 128 * j + 128]
            part = part.astype(jnp.float32) * spread[j]
            sums[j] = part if sums[j] is None else sums[j] + part
    turned = [
        jnp.where(live, jnp.transpose(v, (1, 0)), 0.0).astype(jnp.bfloat16) for v in sums
    ]
    att_ref[:128, :mid] = turned[0]
    att_ref[128:, :mid] = turned[1][:64]
    att_ref[:64, mid:] = turned[1][64:]
    att_ref[64:, mid:] = turned[2]


SMEM = pl.BlockSpec(memory_space=pltpu.SMEM)
VMEM = pl.BlockSpec(memory_space=pltpu.VMEM)
ANY = pl.BlockSpec(memory_space=pl.ANY)
SMALL = pltpu.CompilerParams(vmem_limit_bytes=40 << 20)


def in_vmem(x):
    return pltpu.with_memory_space_constraint(x, pltpu.VMEM)


def in_hbm(x):
    return pltpu.with_memory_space_constraint(x, pltpu.HBM)


def body(stream_x, qkv_weight, short_lengths, cache_owner):
    groups, columns = lax.axis_size("q"), lax.axis_size("y")
    targets = PAIR * columns
    tok_count = stream_x.shape[0]
    group, member, column = lax.axis_index("q"), lax.axis_index("p"), lax.axis_index("y")
    plane = group * PAIR + member
    core = lax.axis_index("c").astype(jnp.int32).reshape(1)
    plane_rows = tok_count * columns
    long_planes = groups * PAIR * 11 // 16
    bounds = boundaries(short_lengths, plane_rows * long_planes)
    stream_end = plane_rows * long_planes + SHORT_SUM

    weight = in_vmem(qkv_weight.T)
    ours = lax.all_gather(stream_x, "x", axis=0, tiled=True)
    theirs = lax.ppermute(ours, "c", [(0, 1), (1, 0)])

    row_ids = (
        plane * plane_rows + column * tok_count + jnp.arange(tok_count, dtype=jnp.int32)
    )
    passed = row_ids[:, None] >= bounds[None, :]
    seg_begin = jnp.max(jnp.where(passed, bounds[None, :], 0), axis=1)
    position = (row_ids - seg_begin).astype(jnp.float32)
    half_dim = HD // 2
    lane = jnp.arange(128, dtype=jnp.int32)
    entry = jnp.where(lane < half_dim, lane, lane - half_dim)
    inverse_freq = rope_base ** (-entry.astype(jnp.float32) / half_dim)
    sign = jnp.where(lane < half_dim, -1.0, jnp.where(lane < HD, 1.0, 0.0))
    angle = position[:, None] * inverse_freq[None, :]
    cosine = jnp.where(lane[None, :] < HD, jnp.cos(angle), 0.0)
    sine = jnp.sin(angle) * sign[None, :]

    owner_row = jnp.where(row_ids < stream_end, cache_owner.reshape(tok_count), -1)
    owner_row = owner_row.astype(jnp.float32)[None, :]

    half = pl.pallas_call(
        half_projection,
        in_specs=[SMEM, VMEM, VMEM],
        out_specs=VMEM,
        out_shape=jax.ShapeDtypeStruct((tok_count, qkv_weight.shape[1]), jnp.float32),
        compiler_params=SMALL,
    )(core, in_vmem(ours), weight)
    queries, key_values = pl.pallas_call(
        rest_projection,
        in_specs=[SMEM] + [VMEM] * 6,
        out_specs=[VMEM, VMEM],
        out_shape=[
            jax.ShapeDtypeStruct((tok_count, 128 + HD), jnp.bfloat16),
            jax.ShapeDtypeStruct((tok_count + 16, 384), jnp.bfloat16),
        ],
        compiler_params=SMALL,
    )(1 - core, in_vmem(theirs), weight, in_vmem(half), in_vmem(cosine), in_vmem(sine), owner_row)

    gathered = lax.all_gather(key_values, "q", axis=0, tiled=True)
    own_queries = lax.all_gather(queries, "y", axis=0, tiled=True)
    other_queries = lax.ppermute(own_queries, "p", [(0, 1), (1, 0)])
    own_queries, short_lengths = lax.optimization_barrier((own_queries, short_lengths))

    bounds = boundaries(short_lengths, plane_rows * long_planes)
    key_ids = (
        (jnp.arange(groups, dtype=jnp.int32) * PAIR + member) * plane_rows + column * tok_count
    )[:, None] + jnp.arange(tok_count, dtype=jnp.int32)[None, :]
    ends = jnp.min(
        jnp.where(bounds[None, None, :] > key_ids[:, :, None], bounds[None, None, :], 1 << 30),
        axis=2,
    )

    info = jnp.stack([group, member, column]).astype(jnp.int32)
    padding = (row_ids[:1] >= stream_end).astype(jnp.int32)
    gathered, own_queries, other_queries, ends, info, padding = lax.optimization_barrier(
        (gathered, own_queries, other_queries, ends, info, padding)
    )

    most = max((long_planes - 1) // PAIR + 1, 2)
    slots = most
    page_rows = groups * CAP
    box_rows = page_rows + tok_count // 2 + 16
    outbox = pl.pallas_call(
        attention,
        in_specs=[SMEM, VMEM, VMEM, VMEM, pl.BlockSpec(memory_space=pltpu.HBM)],
        out_specs=VMEM,
        out_shape=jax.ShapeDtypeStruct((targets, box_rows, 384), jnp.bfloat16),
        scratch_shapes=[
            pltpu.VMEM((groups, tok_count + 16, 384), jnp.bfloat16),
            pltpu.VMEM((plane_rows, 384), jnp.bfloat16),
            pltpu.VMEM((slots, 2, plane_rows, 256), jnp.float32),
            pltpu.VMEM((2, plane_rows, 128), jnp.float32),
            pltpu.VMEM((2, plane_rows, 128), jnp.float32),
            pltpu.VMEM((2, plane_rows, 256), jnp.float32),
            pltpu.SemaphoreType.DMA((groups,)),
        ],
        compiler_params=SMALL,
    )(
        info,
        in_vmem(own_queries),
        in_vmem(other_queries),
        ends,
        gathered.reshape(groups, tok_count + 16, 384),
    )
    received = lax.all_to_all(outbox, ("p", "y"), split_axis=0, concat_axis=0, tiled=True)
    attended, row_lse, kv_cache = pl.pallas_call(
        combine,
        in_specs=[SMEM, VMEM, VMEM],
        out_specs=[VMEM, VMEM, VMEM],
        out_shape=[
            jax.ShapeDtypeStruct((2 * HD, tok_count), jnp.bfloat16),
            jax.ShapeDtypeStruct((2, tok_count), jnp.float32),
            jax.ShapeDtypeStruct((groups, targets, CAP, 384), jnp.bfloat16),
        ],
        compiler_params=SMALL,
    )(
        padding,
        in_vmem(received.reshape(targets, box_rows // CAP, CAP, 384)),
        in_vmem(received),
    )
    return (attended.T, row_lse, kv_cache.reshape(-1, 384))


def solution(mesh):
    seq, head = mesh.devices.shape
    shape = (seq // (MESH_Y * PAIR), PAIR, MESH_Y, head // 2, 2)
    fine = Mesh(mesh.devices.reshape(shape), ("q", "p", "y", "x", "c"))
    seq_axes, head_axes = ("q", "p", "y"), ("x", "c")
    return jax.shard_map(
        body,
        mesh=fine,
        in_specs=(P(seq_axes, head_axes), P(None, head_axes), P(), P(seq_axes, None)),
        out_specs=(P(seq_axes, head_axes), P(head_axes, seq_axes), P(seq_axes, head_axes)),
        check_vma=False,
    )
```

```python
import functools
import math

import jax
import jax.numpy as jnp
from jax import lax
from jax.experimental import pallas as pl
from jax.experimental.pallas import tpu as pltpu
from jax.sharding import Mesh, PartitionSpec as P

HD = 96
CAP = 8
neg_large = -1e30
rope_base = 10000.0
score_scale = 1.0 / math.sqrt(HD)
log2_scale = score_scale * math.log2(math.e)


def boundaries(short_lengths, long_length):
    count = short_lengths.shape[0]
    before = jnp.arange(count)[None, :] < jnp.arange(count + 1)[:, None]
    return jnp.sum(jnp.where(before, short_lengths[None, :], 0), axis=1) + long_length


PAIR = 2
KEYS = 256
SHORT_SUM = 4096
MESH_Y = 4


def lane_ids(shape):
    return lax.broadcasted_iota(jnp.int32, shape, 1)


def block_sum(core, x_ref, w_ref):
    rows = 256
    depth = x_ref.shape[1]
    total = None
    for i in range(x_ref.shape[0] // rows):
        first = pl.multiple_of((2 * i + core) * depth, 128)
        part = lax.dot_general(
            x_ref[i * rows : (i + 1) * rows, :],
            w_ref[:, pl.ds(first, depth)],
            (((1,), (1,)), ((), ())),
            preferred_element_type=jnp.float32,
        )
        total = part if total is None else total + part
    return total


def half_projection(core_ref, x_ref, w_ref, out_ref):
    out_ref[...] = block_sum(core_ref[0], x_ref, w_ref)


def pack_heads(p0, p1, p2, p3):
    lanes = lane_ids(p0.shape)
    r1 = pltpu.roll(p1, 96, 1)
    r2 = pltpu.roll(p2, 64, 1)
    r3 = pltpu.roll(p3, 32, 1)
    return (
        jnp.where(lanes < 96, p0, r1),
        jnp.where(lanes < 64, r1, r2),
        jnp.where(lanes < 32, r2, r3),
    )


def rest_projection(
    core_ref, x_ref, w_ref, first_ref, cos_ref, sin_ref, owner_ref, q_ref, kv_ref
):
    total = first_ref[...] + block_sum(core_ref[0], x_ref, w_ref)
    rows, columns = total.shape
    width = columns + 64
    whole = jnp.concatenate([total, jnp.zeros((rows, 64), jnp.float32)], axis=1)
    cosine = cos_ref[...]
    sine = sin_ref[...]
    lanes = lane_ids((rows, 128))

    def window(first):
        return pltpu.roll(whole, (width - first) % width, 1)[:, :128]

    def rotated(first):
        here = window(first)
        ahead = window(first + 48)
        behind = window((first - 48) % width)
        return here * cosine + jnp.where(lanes < 48, ahead, behind) * sine

    def plain(first):
        return jnp.where(lanes < HD, window(first), 0.0)

    key_values = pack_heads(rotated(96), plain(192), rotated(384), plain(480))
    for i in range(3):
        kv_ref[:rows, 128 * i : 128 * i + 128] = key_values[i].astype(jnp.bfloat16)
    kv_ref[rows:, :rows] = jnp.broadcast_to(owner_ref[...], (16, rows)).astype(jnp.bfloat16)
    kv_ref[rows:, rows:] = jnp.zeros((16, 384 - rows), jnp.bfloat16)
    q0 = rotated(0)
    q1 = rotated(288)
    mid = rows // 2
    queries = pack_heads(q0[:mid], q1[:mid], q0[mid:], q1[mid:])
    for i in range(3):
        q_ref[:, 128 * i : 128 * i + 128] = queries[i].astype(jnp.bfloat16)


def attention(
    info_ref,
    own_ref,
    other_ref,
    ends_ref,
    kv_hbm,
    out_ref,
    kv_ref,
    qs,
    scores,
    peaks,
    totals,
    contexts,
    kv_sems,
):
    group, member, column = info_ref[0], info_ref[1], info_ref[2]
    groups = kv_ref.shape[0]
    rows = MESH_Y * KEYS
    chunk = 256
    targets = out_ref.shape[0]
    page_rows = groups * CAP
    long_planes = 11 * groups * PAIR // 16

    def fetch(k):
        return pltpu.make_async_copy(kv_hbm.at[k], kv_ref.at[k], kv_sems.at[k])

    least = jnp.where(group * PAIR < long_planes, 0, group - 1)

    def start_fetch(k, carry):
        fetch(k).start()
        return carry

    def wait_fetch(k, carry):
        fetch(k).wait()
        return carry

    lax.fori_loop(least, group + 1, start_fetch, 0)
    lax.fori_loop(0, least, start_fetch, 0)
    lax.fori_loop(group + 1, groups, start_fetch, 0)

    key_cols = (slice(0, 128), slice(128, 384))
    value_cols = (slice(0, 256), slice(256, 384))
    value_width = (256, 128)
    parts = [
        (head, slice(first, first + chunk), first)
        for head in range(2)
        for first in range(0, rows, chunk)
    ]
    lanes = lane_ids((chunk, 128))

    def one_plane(h, q_ref, waits):
        plane = group * PAIR + h
        is_long = plane < long_planes
        low = jnp.where(is_long, 0, group - 1)
        masked_low = jnp.where(is_long, group, group - 1)

        for first in range(0, rows, chunk):
            mid = chunk // 2
            short_lanes = lane_ids((mid, 128))
            block = q_ref[first // 2 : first // 2 + mid, :].astype(jnp.float32)
            for side in range(2):
                begin = 2 * HD * side
                q0 = pltpu.roll(block, (384 - begin) % 384, 1)[:, :128]
                q1 = pltpu.roll(block, (384 - begin - HD + 64) % 384, 1)[:, :256]
                span = slice(first + side * mid, first + side * mid + mid)
                qs[span, :128] = jnp.where(short_lanes < HD, q0, 0.0).astype(jnp.bfloat16)
                qs[span, 128:256] = jnp.where(short_lanes < 64, 0.0, q1[:, :128]).astype(
                    jnp.bfloat16
                )
                qs[span, 256:] = jnp.where(short_lanes < 32, q1[:, 128:], 0.0).astype(jnp.bfloat16)

        if waits:
            lax.fori_loop(least, group + 1, wait_fetch, 0)

        def score(k, masked, fresh=False):
            for head, span, first in parts:
                s = lax.dot_general(
                    qs[span, key_cols[head]],
                    kv_ref[k, :KEYS, key_cols[head]],
                    (((1,), (1,)), ((), ())),
                    preferred_element_type=jnp.float32,
                )
                if masked:
                    shape = (chunk, KEYS)
                    row_ids = plane * rows + first + lax.broadcasted_iota(jnp.int32, shape, 0)
                    key_ids = (
                        (k * PAIR + member) * rows
                        + column * KEYS
                        + lax.broadcasted_iota(jnp.int32, shape, 1)
                    )
                    allowed = (key_ids <= row_ids) & (row_ids < ends_ref[pl.ds(k, 1), :])
                    s = jnp.where(allowed, s, neg_large)
                scores[k - low, head, span, :] = s
                top = jnp.maximum(s[:, :128], s[:, 128:])
                if not fresh:
                    top = jnp.maximum(peaks[head, span, :], top)
                peaks[head, span, :] = top

        def free_step(k, carry):
            score(k, False)
            return carry

        def masked_step(k, carry):
            score(k, True)
            return carry

        score(group, True, True)
        lax.fori_loop(low, masked_low, free_step, 0)
        lax.fori_loop(masked_low, group, masked_step, 0)

        tops = []
        for head, span, first in parts:
            top = jnp.max(peaks[head, span, :], axis=1, keepdims=True)
            tops.append(top)
            peaks[head, span, :] = jnp.broadcast_to(top * log2_scale, (chunk, 128))

        def weigh(k, fresh):
            for head, span, first in parts:
                shift = peaks[head, span, :]
                s = scores[k - low, head, span, :]
                left = jnp.exp2(s[:, :128] * log2_scale - shift)
                right = jnp.exp2(s[:, 128:] * log2_scale - shift)
                total = left + right
                p = jnp.concatenate([left.astype(jnp.bfloat16), right.astype(jnp.bfloat16)], axis=1)
                context = jnp.dot(
                    p, kv_ref[k, :KEYS, value_cols[head]], preferred_element_type=jnp.float32
                )
                if not fresh:
                    total = totals[head, span, :] + total
                    context = contexts[head, span, : value_width[head]] + context
                totals[head, span, :] = total
                contexts[head, span, : value_width[head]] = context

        def weigh_step(k, carry):
            weigh(k, False)
            return carry

        weigh(group, True)
        lax.fori_loop(low, group, weigh_step, 0)

        for first in range(0, rows, chunk):
            span = slice(first, first + chunk)
            found = []
            spread = jnp.zeros((chunk, 128), jnp.float32)
            for head in range(2):
                top = tops[head * (rows // chunk) + first // chunk]
                denominator = jnp.sum(totals[head, span, :], axis=1, keepdims=True)
                if head == 0:
                    left = pltpu.roll(contexts[head, span, :128], 32, 1)
                    right = pltpu.roll(contexts[head, span, 128:], 32, 1)
                    context = jnp.where(lanes < 32, left, right)
                else:
                    context = pltpu.roll(contexts[head, span, :128], 96, 1)
                found.append(jnp.where(lanes < HD, context / denominator, 0.0))
                spread = jnp.where(lanes == 2 * head, top, spread)
                spread = jnp.where(lanes == 2 * head + 1, denominator, spread)
            turned = jnp.transpose(spread, (1, 0))
            pieces = []
            for head in range(2):
                lse = turned[2 * head : 2 * head + 1] * score_scale + jnp.log(
                    turned[2 * head + 1 : 2 * head + 2]
                )
                coarse = lse.astype(jnp.bfloat16).astype(jnp.float32)
                middle = (lse - coarse).astype(jnp.bfloat16).astype(jnp.float32)
                pieces += [coarse, middle, lse - coarse - middle]
            pieces.append(jnp.zeros((10, chunk), jnp.float32))
            pieces = jnp.concatenate(pieces, axis=0).astype(jnp.bfloat16)
            target = h * MESH_Y + first // KEYS
            mid = chunk // 2
            packed = pack_heads(found[0][:mid], found[1][:mid], found[0][mid:], found[1][mid:])
            for i in range(3):
                out_ref[target, page_rows : page_rows + mid, 128 * i : 128 * i + 128] = packed[
                    i
                ].astype(jnp.bfloat16)
            tail = slice(page_rows + mid, page_rows + mid + 16)
            out_ref[target, tail, :chunk] = pieces
            out_ref[target, tail, chunk:] = jnp.zeros((16, 384 - chunk), jnp.bfloat16)

    one_plane(member, own_ref, True)
    one_plane(1 - member, other_ref, False)

    lax.fori_loop(0, least, wait_fetch, 0)
    lax.fori_loop(group + 1, groups, wait_fetch, 0)
    shape = (targets * 16, KEYS)
    row = lax.broadcasted_iota(jnp.int32, shape, 0)
    key = lax.broadcasted_iota(jnp.int32, shape, 1)
    same_place = (row & 7) == (key & 7)
    parity = (row >> 3) & 1
    owner = (group * targets + (row >> 4)).astype(jnp.float32)
    for two in range(groups // 2):
        total = None
        for n in range(2):
            k = 2 * two + n
            owners = kv_ref[k, KEYS : KEYS + 16, :KEYS].astype(jnp.float32)[:1]
            chosen = (owners == owner) & same_place & (parity == n)
            picked = jnp.dot(
                jnp.where(chosen, 1.0, 0.0).astype(jnp.bfloat16),
                kv_ref[k, :KEYS, :],
                preferred_element_type=jnp.float32,
            )
            total = picked if total is None else total + picked
        total = total.astype(jnp.bfloat16)
        for t in range(targets):
            out_ref[t, 16 * two : 16 * two + 16, :] = total[16 * t : 16 * t + 16]


def combine(flag_ref, pages_ref, got_ref, att_ref, lse_ref, cache_ref):
    count = got_ref.shape[0]
    groups = cache_ref.shape[0]
    base = groups * CAP
    for t in range(count):
        cache_ref[:, t] = pages_ref[t, :groups]
    live = flag_ref[0] == 0
    mid = KEYS // 2
    shares = []
    for head in range(2):
        lses = []
        for i in range(count):
            rows = got_ref[i, base + mid : base + mid + 16, :KEYS].astype(jnp.float32)
            first = 3 * head
            lses.append(
                rows[first : first + 1] + rows[first + 1 : first + 2] + rows[first + 2 : first + 3]
            )
        lses = jnp.concatenate(lses, axis=0)
        peak = jnp.max(lses, axis=0, keepdims=True)
        weights = jnp.exp(lses - peak)
        total = jnp.sum(weights, axis=0, keepdims=True)
        shares.append(weights / total)
        lse_ref[head : head + 1, :] = jnp.where(live, peak + jnp.log(total), 0.0)
    shares.append(jnp.zeros((128 - 2 * count, KEYS), jnp.float32))
    shares = jnp.transpose(jnp.concatenate(shares, axis=0), (1, 0))
    lanes = lane_ids((mid, 128))
    sums = [None] * 3
    for i in range(count):
        near0, near1 = shares[:mid, i : i + 1], shares[:mid, count + i : count + i + 1]
        far0, far1 = shares[mid:, i : i + 1], shares[mid:, count + i : count + i + 1]
        spread = (
            jnp.where(lanes < 96, near0, near1),
            jnp.where(lanes < 64, near1, far0),
            jnp.where(lanes < 32, far0, far1),
        )
        for j in range(3):
            part = got_ref[i, base : base + mid, 128 * j : 128 * j + 128]
            part = part.astype(jnp.float32) * spread[j]
            sums[j] = part if sums[j] is None else sums[j] + part
    turned = [
        jnp.where(live, jnp.transpose(v, (1, 0)), 0.0).astype(jnp.bfloat16) for v in sums
    ]
    att_ref[:128, :mid] = turned[0]
    att_ref[128:, :mid] = turned[1][:64]
    att_ref[:64, mid:] = turned[1][64:]
    att_ref[64:, mid:] = turned[2]


SMEM = pl.BlockSpec(memory_space=pltpu.SMEM)
VMEM = pl.BlockSpec(memory_space=pltpu.VMEM)
ANY = pl.BlockSpec(memory_space=pl.ANY)
SMALL = pltpu.CompilerParams(vmem_limit_bytes=40 << 20)


def in_vmem(x):
    return pltpu.with_memory_space_constraint(x, pltpu.VMEM)


def in_hbm(x):
    return pltpu.with_memory_space_constraint(x, pltpu.HBM)


def body(stream_x, qkv_weight, short_lengths, cache_owner):
    groups, columns = lax.axis_size("q"), lax.axis_size("y")
    targets = PAIR * columns
    tok_count = stream_x.shape[0]
    group, member, column = lax.axis_index("q"), lax.axis_index("p"), lax.axis_index("y")
    plane = group * PAIR + member
    core = lax.axis_index("c").astype(jnp.int32).reshape(1)
    plane_rows = tok_count * columns
    long_planes = groups * PAIR * 11 // 16
    bounds = boundaries(short_lengths, plane_rows * long_planes)
    stream_end = plane_rows * long_planes + SHORT_SUM

    weight = in_vmem(qkv_weight.T)
    ours = lax.all_gather(stream_x, "x", axis=0, tiled=True)
    theirs = lax.ppermute(ours, "c", [(0, 1), (1, 0)])

    row_ids = (
        plane * plane_rows + column * tok_count + jnp.arange(tok_count, dtype=jnp.int32)
    )
    passed = row_ids[:, None] >= bounds[None, :]
    seg_begin = jnp.max(jnp.where(passed, bounds[None, :], 0), axis=1)
    position = (row_ids - seg_begin).astype(jnp.float32)
    half_dim = HD // 2
    lane = jnp.arange(128, dtype=jnp.int32)
    entry = jnp.where(lane < half_dim, lane, lane - half_dim)
    inverse_freq = rope_base ** (-entry.astype(jnp.float32) / half_dim)
    sign = jnp.where(lane < half_dim, -1.0, jnp.where(lane < HD, 1.0, 0.0))
    angle = position[:, None] * inverse_freq[None, :]
    cosine = jnp.where(lane[None, :] < HD, jnp.cos(angle), 0.0)
    sine = jnp.sin(angle) * sign[None, :]

    owner_row = jnp.where(row_ids < stream_end, cache_owner.reshape(tok_count), -1)
    owner_row = owner_row.astype(jnp.float32)[None, :]

    half = pl.pallas_call(
        half_projection,
        in_specs=[SMEM, VMEM, VMEM],
        out_specs=VMEM,
        out_shape=jax.ShapeDtypeStruct((tok_count, qkv_weight.shape[1]), jnp.float32),
        compiler_params=SMALL,
    )(core, in_vmem(ours), weight)
    queries, key_values = pl.pallas_call(
        rest_projection,
        in_specs=[SMEM] + [VMEM] * 6,
        out_specs=[VMEM, VMEM],
        out_shape=[
            jax.ShapeDtypeStruct((tok_count // 2, 384), jnp.bfloat16),
            jax.ShapeDtypeStruct((tok_count + 16, 384), jnp.bfloat16),
        ],
        compiler_params=SMALL,
    )(1 - core, in_vmem(theirs), weight, in_vmem(half), in_vmem(cosine), in_vmem(sine), owner_row)

    gathered = lax.all_gather(key_values, "q", axis=0, tiled=True)
    own_queries = lax.all_gather(queries, "y", axis=0, tiled=True)
    other_queries = lax.ppermute(own_queries, "p", [(0, 1), (1, 0)])
    own_queries, short_lengths = lax.optimization_barrier((own_queries, short_lengths))

    bounds = boundaries(short_lengths, plane_rows * long_planes)
    key_ids = (
        (jnp.arange(groups, dtype=jnp.int32) * PAIR + member) * plane_rows + column * tok_count
    )[:, None] + jnp.arange(tok_count, dtype=jnp.int32)[None, :]
    ends = jnp.min(
        jnp.where(bounds[None, None, :] > key_ids[:, :, None], bounds[None, None, :], 1 << 30),
        axis=2,
    )

    info = jnp.stack([group, member, column]).astype(jnp.int32)
    padding = (row_ids[:1] >= stream_end).astype(jnp.int32)
    gathered, own_queries, other_queries, ends, info, padding = lax.optimization_barrier(
        (gathered, own_queries, other_queries, ends, info, padding)
    )

    most = max((long_planes - 1) // PAIR + 1, 2)
    slots = most
    page_rows = groups * CAP
    box_rows = page_rows + tok_count // 2 + 16
    outbox = pl.pallas_call(
        attention,
        in_specs=[SMEM, VMEM, VMEM, VMEM, pl.BlockSpec(memory_space=pltpu.HBM)],
        out_specs=VMEM,
        out_shape=jax.ShapeDtypeStruct((targets, box_rows, 384), jnp.bfloat16),
        scratch_shapes=[
            pltpu.VMEM((groups, tok_count + 16, 384), jnp.bfloat16),
            pltpu.VMEM((plane_rows, 384), jnp.bfloat16),
            pltpu.VMEM((slots, 2, plane_rows, 256), jnp.float32),
            pltpu.VMEM((2, plane_rows, 128), jnp.float32),
            pltpu.VMEM((2, plane_rows, 128), jnp.float32),
            pltpu.VMEM((2, plane_rows, 256), jnp.float32),
            pltpu.SemaphoreType.DMA((groups,)),
        ],
    )(
        info,
        in_vmem(own_queries),
        in_vmem(other_queries),
        ends,
        gathered.reshape(groups, tok_count + 16, 384),
    )
    received = lax.all_to_all(outbox, ("p", "y"), split_axis=0, concat_axis=0, tiled=True)
    attended, row_lse, kv_cache = pl.pallas_call(
        combine,
        in_specs=[SMEM, VMEM, VMEM],
        out_specs=[VMEM, VMEM, VMEM],
        out_shape=[
            jax.ShapeDtypeStruct((2 * HD, tok_count), jnp.bfloat16),
            jax.ShapeDtypeStruct((2, tok_count), jnp.float32),
            jax.ShapeDtypeStruct((groups, targets, CAP, 384), jnp.bfloat16),
        ],
        compiler_params=SMALL,
    )(
        padding,
        in_vmem(received.reshape(targets, box_rows // CAP, CAP, 384)),
        in_vmem(received),
    )
    return (attended.T, row_lse, kv_cache.reshape(-1, 384))


def solution(mesh):
    seq, head = mesh.devices.shape
    shape = (seq // (MESH_Y * PAIR), PAIR, MESH_Y, head // 2, 2)
    fine = Mesh(mesh.devices.reshape(shape), ("q", "p", "y", "x", "c"))
    seq_axes, head_axes = ("q", "p", "y"), ("x", "c")
    return jax.shard_map(
        body,
        mesh=fine,
        in_specs=(P(seq_axes, head_axes), P(None, head_axes), P(), P(seq_axes, None)),
        out_specs=(P(seq_axes, head_axes), P(head_axes, seq_axes), P(seq_axes, head_axes)),
        check_vma=False,
    )
```
